128 devices in a mesh: dp: 32 (over x, z, core), rep: 4 (over y).
Axes of the slice: x: 4, y: 4, z: 4, core: 2. Of those that a mesh axis runs over, the one named last changes fastest.
Arguments:
- events: bfloat16 [65536, 512], P(('dp', 'rep')), may hold values from -6 to 6
- grad_out: bfloat16 [65536, 512], P(('dp', 'rep')), may hold values from -15 to 15
- w_uvqk: bfloat16 [512, 2048], replicated, may hold values from -0.25 to 0.25
- w_out: bfloat16 [512, 512], replicated, may hold values from -0.25 to 0.25
- send_place: int32 [128, 512], P(('dp', 'rep')), may hold values from 0 to 1023, as said below
- send_counts: int32 [128, 32], P(('dp', 'rep')), may hold values from 0 to 32, as said below
- user_ids: int32 [128, 512], P(('dp', 'rep')), may hold values from 0 to 15, never falling along the last dimension, each value on 1 to 256 neighbouring positions
Outputs:
- grad_events: bfloat16 [65536, 512], P(('dp', 'rep'))
- grad_w_uvqk: float32 [512, 2048], P(None, 'dp')
- grad_w_out: float32 [512, 512], P(None, 'dp')
The draws below stay inside these ranges and needn't reach their ends.
Inputs may be any that keep to these rules, and one draw needn't show every extreme that they name: `send_counts`: row d * 4 + r gives, for each owner o of group r, how many events device (d, r) sends there; each row sums to 512, and the counts one owner receives from the 32 devices of its group also sum to 512. `send_place`: an event bound for owner o has place o * 32 + j, where j runs from 0 to that owner's count minus 1 over the device's events bound for o; each place at most once on a device. `user_ids`: each row lists an owner's users in the owner's order of events; ids never fall.
All inputs are finite; a program needn't handle non-finite values.
Results may differ from the reference program's by a relative error of at most 0.02.
Values may be sent and summed in bfloat16 or wider, within the bound.
A program may use at most 192 MiB of HBM per device.

```python
import math
import jax
import jax.numpy as jnp
import numpy as np
from jax import lax

D = 512
HEADS = 8
EV_DEV = 512
CAP = 32
USERS = 16
LEN_MOST = 256
EVENTS = 65536
N_DP = 32
N_REP = 4


def routing_tables(key):
    owners = N_DP
    groups = N_REP
    mean_count = EV_DEV // N_DP
    deltas = jax.random.randint(jax.random.fold_in(key, 11), (groups, owners // 2), 0, mean_count // 2 + 1)
    deltas = deltas.at[:, 0].set(mean_count)
    profile = jnp.stack([mean_count + deltas, mean_count - deltas], axis=-1).reshape(groups, owners)
    shifts = jax.random.randint(jax.random.fold_in(key, 12), (groups,), 0, owners)
    rolled = (jnp.arange(owners)[None, :] - shifts[:, None]) % owners
    profile = jnp.take_along_axis(profile, rolled, axis=1)
    blocks = jnp.arange(owners * groups)
    source = blocks // groups
    group = blocks % groups
    column = (jnp.arange(owners)[None, :] - source[:, None]) % owners
    counts = profile[group[:, None], column].astype(jnp.int32)
    ends = jnp.cumsum(counts, axis=1).astype(jnp.int32)
    starts = ends - counts
    target_positions = jnp.arange(EV_DEV, dtype=jnp.int32)
    owner_of = jnp.sum((target_positions[None, :, None] >= ends[:, None, :]).astype(jnp.int32), axis=2)
    first = jnp.take_along_axis(starts, owner_of, axis=1)
    slots = owner_of * CAP + target_positions[None, :] - first
    keys = jax.random.split(jax.random.fold_in(key, 13), owners * groups)
    sorting_orders = jax.vmap(lambda single: jax.random.permutation(single, EV_DEV))(keys)
    slots = jnp.take_along_axis(slots, sorting_orders, axis=1)
    return (counts, slots.astype(jnp.int32))


def draw_send_counts(key, part):
    return routing_tables(key)[0]


def draw_send_place(key, part):
    return routing_tables(key)[1]


def zero_rows(key):
    counts, slots = routing_tables(key)
    blocks = N_DP * N_REP
    owner_of = slots // CAP
    within = slots - owner_of * CAP
    last_of = jnp.take_along_axis(counts, owner_of, axis=1) - 1
    picked = jax.random.randint(jax.random.fold_in(key, 14), (blocks, N_DP), 0, 4) == 0
    device_rows = jnp.arange(blocks, dtype=jnp.int32)
    picked = picked | (jnp.arange(N_DP, dtype=jnp.int32)[None, :] == (device_rows % N_DP)[:, None])
    chosen = jnp.take_along_axis(picked, owner_of, axis=1) & (within == last_of)
    keep = jnp.where(chosen, 0.0, 1.0).astype(jnp.float32)
    return keep.reshape(EVENTS, 1)


def draw_events(key, part):
    value_key = jax.random.fold_in(key, 21)
    values = jax.random.truncated_normal(value_key, -6.0, 6.0, (EVENTS, D), jnp.float32)
    return (values * zero_rows(key)).astype(jnp.bfloat16)


def draw_grad_out(key, part):
    value_key = jax.random.fold_in(key, 22)
    blocks = N_DP * N_REP
    values = jax.random.truncated_normal(value_key, -6.0, 6.0, (EVENTS, D), jnp.float32)
    pairing = jax.random.permutation(jax.random.fold_in(key, 23), N_DP)
    device_rows = jnp.arange(blocks, dtype=jnp.int32)
    target_block = pairing[(device_rows // N_REP + device_rows % N_REP) % N_DP]
    column_block = jnp.arange(D, dtype=jnp.int32) // (D // N_DP)
    boost = jnp.where(column_block[None, :] == target_block[:, None], 2.5, 1.0).astype(jnp.float32)
    values = (values.reshape(blocks, EV_DEV, D) * boost[:, None, :]).reshape(EVENTS, D)
    return (values * zero_rows(key)).astype(jnp.bfloat16)


def length_profile(count, total, most, slope):
    loads = [(1 << 20) // math.isqrt(grade ** slope) + 1 for grade in range(2, count + 1)]
    surplus, given = total - most - (count - 1), [1] * (count - 1)
    while surplus > 0:
        candidates = [i for i in range(count - 1) if given[i] < most]
        pool, budget = sum([loads[i] for i in candidates]), surplus
        for i in candidates:
            addition = min(most - given[i], max(1, budget * loads[i] // pool), surplus)
            given[i] = given[i] + addition
            surplus = surplus - addition
    return np.array([most] + given)


def ragged_sizes(stream_key, amount, total, most, slope):
    if amount == 2:
        one = jax.random.randint(stream_key, (), max(1, total - most), min(most, total - 1) + 1)
        return jnp.stack([one, total - one])
    sizes = jnp.asarray(length_profile(amount, total, most, slope), jnp.int32)
    couples = (amount - 1) // 2
    giver, taker = sizes[1:1 + 2 * couples:2], sizes[2:2 + 2 * couples:2]
    slack = jnp.minimum(giver - 1, most - taker)
    passed = jax.random.randint(jax.random.fold_in(stream_key, 1), (couples,), 0, 1 << 20) % (slack + 1)
    sizes = sizes.at[1:1 + 2 * couples:2].set(giver - passed).at[2:2 + 2 * couples:2].set(taker + passed)
    return sizes[jax.random.permutation(jax.random.fold_in(stream_key, 2), amount)]


def centred(own_key, dims, scale, most, kind=jnp.bfloat16):
    values = jax.random.normal(own_key, dims, jnp.float32) * scale
    return jnp.minimum(jnp.maximum(values, -most), most).astype(kind)


def setup_inputs(seed: int = 0) -> dict:
    seeds = jax.random.split(jax.random.key(seed), 8)
    return {
        "events": draw_events(jax.random.fold_in(seeds[7], 71), 0),
        "grad_out": draw_grad_out(jax.random.fold_in(seeds[7], 71), 0),
        "w_uvqk": centred(seeds[2], (D, 4 * D), D ** -0.5, 0.25),
        "w_out": centred(seeds[3], (D, D), D ** -0.5, 0.25),
        "send_place": draw_send_place(jax.random.fold_in(seeds[7], 71), 0),
        "send_counts": draw_send_counts(jax.random.fold_in(seeds[7], 71), 0),
        "user_ids": jax.vmap(lambda own: jnp.searchsorted(jnp.cumsum(ragged_sizes(own, USERS, EV_DEV, LEN_MOST, 2)), jnp.arange(EV_DEV), side="right"))(jax.random.split(seeds[6], (N_DP * N_REP))).reshape((N_DP * N_REP, EV_DEV)).astype(jnp.int32),
    }


EPSILON = 1e-05

def normalized_row_block(values):
    center = values - lax.optimization_barrier(jnp.mean(values, axis=-1, keepdims=True))
    spread = lax.optimization_barrier(jnp.mean(center * center, axis=-1, keepdims=True))
    return center * lax.rsqrt(spread + EPSILON)

def hstu_layer(event_row_block, input_weight_matrix, weight_out, allowed):
    width = weight_out.shape[0]
    count = event_row_block.shape[0]
    head_size = width // HEADS
    normalized_input = normalized_row_block(event_row_block.astype(jnp.float32)).astype(jnp.bfloat16)
    activation_value = jax.nn.silu(jnp.dot(normalized_input, input_weight_matrix, preferred_element_type=jnp.float32)).astype(jnp.bfloat16)
    gate_u = activation_value[:, :width]
    values = activation_value[:, width:2 * width].reshape(count, HEADS, head_size)
    queries = activation_value[:, 2 * width:3 * width].reshape(count, HEADS, head_size)
    keys = activation_value[:, 3 * width:].reshape(count, HEADS, head_size)
    scores = jnp.einsum('qhd,khd->hqk', queries.astype(jnp.float32), keys.astype(jnp.float32)) * head_size ** (-0.5)
    weights = (jax.nn.silu(scores) * allowed[None]).astype(jnp.bfloat16)
    attended = jnp.einsum('hqk,khd->qhd', weights.astype(jnp.float32), values.astype(jnp.float32)).reshape(count, width)
    gated = (normalized_row_block(attended) * gate_u.astype(jnp.float32)).astype(jnp.bfloat16)
    return event_row_block.astype(jnp.float32) + jnp.dot(gated, weight_out, preferred_element_type=jnp.float32)

def owner_grads(event_row_block, cotangent, input_weight_matrix, weight_out, allowed):
    result, pullback = jax.vjp(lambda first, second, third: hstu_layer(first, second, third, allowed), event_row_block, input_weight_matrix, weight_out)
    return pullback(cotangent.astype(jnp.float32))

def compact_index(counts_in, owned, capacity):
    ends = jnp.cumsum(counts_in).astype(jnp.int32)
    starts = (ends - counts_in).astype(jnp.int32)
    target_positions = jnp.arange(owned, dtype=jnp.int32)
    source = lax.optimization_barrier(jnp.sum((target_positions[:, None] >= ends[None, :]).astype(jnp.int32), axis=1)).astype(jnp.int32)
    onehot = (jnp.arange(counts_in.shape[0], dtype=jnp.int32)[None, :] == source[:, None]).astype(jnp.int32)
    first = lax.optimization_barrier(jnp.sum(onehot * starts[None, :], axis=1)).astype(jnp.int32)
    return (source * capacity + target_positions - first).astype(jnp.int32)

def reference(events, grad_out, w_uvqk, w_out, send_place, send_counts, user_ids):
    owners = N_DP
    groups = N_REP
    width = D

    def spread_rows(event_row_block):
        blocks = event_row_block.reshape(owners * groups, EV_DEV, width)
        buffers = jax.vmap(lambda part, place: jnp.zeros((owners * CAP, width), part.dtype).at[place].set(part))(blocks, send_place)
        buffers = buffers.reshape(owners, groups, owners, CAP, width)
        return buffers.transpose(2, 1, 0, 3, 4).reshape(owners * groups, owners * CAP, width)
    recv_x = spread_rows(events)
    recv_dy = spread_rows(grad_out)
    count_cols = send_counts.reshape(owners, groups, owners).transpose(2, 1, 0).reshape(owners * groups, owners)

    def step(carry, inputs):
        rows_x, rows_dy, counts_in, users = inputs
        order_index = compact_index(counts_in, EV_DEV, CAP)
        owned_x = jnp.take(rows_x, order_index, axis=0)
        owned_dy = jnp.take(rows_dy, order_index, axis=0)
        target_positions = jnp.arange(EV_DEV, dtype=jnp.int32)
        allowed = ((users[:, None] == users[None, :]) & (target_positions[None, :] <= target_positions[:, None])).astype(jnp.float32)
        grad_x, grad_in, grad_outw = owner_grads(owned_x, owned_dy, w_uvqk, w_out, allowed)
        padded = jnp.zeros((owners * CAP, width), jnp.bfloat16).at[order_index].set(grad_x)
        return ((carry[0] + grad_in.astype(jnp.float32), carry[1] + grad_outw.astype(jnp.float32)), padded)
    start = (jnp.zeros((width, 4 * width), jnp.float32), jnp.zeros((width, width), jnp.float32))
    sums, padded_all = lax.scan(step, start, (recv_x, recv_dy, count_cols, user_ids))
    back = padded_all.reshape(owners, groups, owners, CAP, width).transpose(2, 1, 0, 3, 4)
    back = back.reshape(owners * groups, owners * CAP, width)
    grad_events = jax.vmap(lambda buffer, place: jnp.take(buffer, place, axis=0))(back, send_place)
    return (grad_events.reshape(owners * groups * EV_DEV, width), sums[0], sums[1])
```

```python
import jax
import jax.numpy as jnp
from jax import lax
from jax.experimental import pallas as pl
from jax.experimental.pallas import tpu as pltpu
from jax.sharding import PartitionSpec as P

HEADS = 8
EPSILON = 1e-05
F32 = jnp.float32
BF16 = jnp.bfloat16
I32 = jnp.int32
MESH = pl.DeviceIdType.MESH
N = 512
DP = 32
REP = 4
CAP = 32
SLOTS = 1024
CHIPS = 16
VMEM_LIMIT = 62 * 1024 * 1024


def dot(a, b):
    return jnp.dot(a, b, preferred_element_type=F32)


def dot_nt(a, b):
    return lax.dot_general(a, b, (((1,), (1,)), ((), ())), preferred_element_type=F32)


def iota(shape, dim):
    return lax.broadcasted_iota(I32, shape, dim)


def onehot(mask):
    return jnp.where(mask, 1.0, 0.0).astype(BF16)


def column_of(row, width):
    return jnp.transpose(jnp.broadcast_to(row, (128, width)))


def position():
    me = lax.axis_index("dp")
    return me, lax.axis_index("rep")


def remote(src, dst, send, recv, dp, rep):
    return pltpu.make_async_remote_copy(
        src_ref=src,
        dst_ref=dst,
        send_sem=send,
        recv_sem=recv,
        device_id=(dp, rep),
        device_id_type=MESH,
    )


def group_signal(barrier, me, rep):
    @pl.loop(1, DP)
    def _(i):
        peer = lax.rem(me + i, DP)
        pl.semaphore_signal(barrier, 1, device_id=(peer, rep), device_id_type=MESH)


def pack(place_ref, rows_ref, out_ref):
    place = place_ref[...]
    for chunk in range(4):
        hot = onehot(iota((256, N), 0) + 256 * chunk == place)
        out_ref[8 * chunk : 8 * chunk + 8] = (
            dot(hot, rows_ref[...]).astype(BF16).reshape(8, CAP, N)
        )


def send_blocks(src, dst, send, recv, local, me, rep):
    @pl.loop(1, DP)
    def _(i):
        peer = lax.rem(me + i, DP)
        remote(src.at[peer], dst.at[me], send.at[peer], recv.at[me], peer, rep).start()

    pltpu.make_async_copy(src.at[me], dst.at[me], local).start()


def wait_blocks(src, dst, send, recv, local, me, rep):
    @pl.loop(1, DP)
    def _(i):
        peer = lax.rem(me + i, DP)
        remote(src.at[peer], dst.at[peer], send.at[peer], recv.at[peer], peer, rep).wait()

    pltpu.make_async_copy(src.at[me], dst.at[me], local).wait()


def send_counts_row(src, dst, send, recv, local, me, rep):
    @pl.loop(1, DP)
    def _(i):
        peer = lax.rem(me + i, DP)
        remote(src, dst.at[me], send.at[peer], recv.at[me], peer, rep).start()

    pltpu.make_async_copy(src, dst.at[me], local).start()


def wait_counts_row(src, dst, send, recv, local, me, rep):
    @pl.loop(1, DP)
    def _(i):
        peer = lax.rem(me + i, DP)
        remote(src, dst.at[peer], send.at[peer], recv.at[peer], peer, rep).wait()

    pltpu.make_async_copy(src, dst.at[me], local).wait()


def dispatch_kernel(
    ev, go, place, cnt, rx, ry, ct, sx, sy, xs, xr, ys, yr, cs, cr, loc
):
    me, rep = position()
    barrier = pltpu.get_barrier_semaphore()
    group_signal(barrier, me, rep)
    pack(place, ev, sx)
    pl.semaphore_wait(barrier, DP - 1)
    send_counts_row(cnt, ct, cs, cr, loc.at[0], me, rep)
    send_blocks(sx, rx, xs, xr, loc.at[1], me, rep)
    pack(place, go, sy)
    send_blocks(sy, ry, ys, yr, loc.at[2], me, rep)
    wait_counts_row(cnt, ct, cs, cr, loc.at[0], me, rep)
    wait_blocks(sx, rx, xs, xr, loc.at[1], me, rep)
    wait_blocks(sy, ry, ys, yr, loc.at[2], me, rep)


def slot_positions(ct):
    me = lax.axis_index("dp")
    table = ct[:, 0, :]
    mine = jnp.where(iota((DP, DP), 1) == me, table, 0).astype(F32)
    counts = jnp.sum(mine, axis=1, keepdims=True)
    source = iota((DP, SLOTS), 0)
    slot_source = iota((DP, SLOTS), 1) // CAP
    start = jnp.sum(jnp.where(source < slot_source, counts, 0.0), axis=0, keepdims=True)
    count = jnp.sum(jnp.where(source == slot_source, counts, 0.0), axis=0, keepdims=True)
    within = lax.rem(iota((1, SLOTS), 1), CAP).astype(F32)
    return jnp.where(within < count, start + within, -1.0)


def compact(pos, rows_ref, out_ref):
    rows = rows_ref[...].reshape(SLOTS, N)
    for chunk in range(2):
        index = (iota((256, SLOTS), 0) + 256 * chunk).astype(F32)
        hot = onehot(index == pos)
        out_ref[256 * chunk : 256 * chunk + 256] = dot(hot, rows).astype(BF16)


def centred(values):
    center = values - jnp.mean(values, axis=-1, keepdims=True)
    spread = jnp.mean(center * center, axis=-1, keepdims=True)
    scale = lax.rsqrt(spread + EPSILON)
    return center * scale, scale


def norm_grad(grad, normed, scale):
    lead = jnp.mean(grad, axis=-1, keepdims=True)
    along = jnp.mean(grad * normed, axis=-1, keepdims=True)
    return scale * (grad - lead - normed * along)


def sigmoid(x):
    return 0.5 * jnp.tanh(0.5 * x) + 0.5


def projection(xh, w, act, slope):
    @pl.loop(0, 8)
    def _(j):
        cols = pl.ds(pl.multiple_of(256 * j, 256), 256)
        pre = dot(xh[...], w[:, cols])
        sig = sigmoid(pre)
        silu = pre * sig
        act[:, cols] = silu.astype(BF16)
        slope[:, cols] = (sig + silu * (1.0 - sig)).astype(BF16)


def allowed_mask(users, mask):
    row = users[...].astype(F32)
    column = column_of(row, N)
    for b in range(4):
        keys = slice(128 * b, 128 * b + 128)
        same = column == row[:, keys]
        causal = iota((N, 128), 1) + 128 * b <= iota((N, 128), 0)
        mask[:, keys] = onehot(same & causal)


def half_lanes(hh):
    return jnp.where(iota((1, 128), 1) // 64 == hh, 1.0, 0.0)


def attention(act, mask, wt, gs, att):
    @pl.loop(0, HEADS // 2)
    def _(p):
        off = pl.multiple_of(128 * p, 128)
        v = act[:, pl.ds(512 + off, 128)]
        q = act[:, pl.ds(1024 + off, 128)]
        k = act[:, pl.ds(1536 + off, 128)]
        for t in range(2):
            rows = slice(256 * t, 256 * t + 256)
            nk = 256 * (t + 1)
            total = None
            for hh in range(2):
                lanes = half_lanes(hh)
                qm = q[rows] * lanes.astype(BF16)
                half = dot_nt(qm, k[:nk]) * 0.0625
                th = jnp.tanh(half)
                silu = half + half * th
                sig = 0.5 + 0.5 * th
                grad = (sig + silu * (1.0 - sig)) * 0.125
                ok = mask[rows, :nk]
                weights = silu.astype(BF16) * ok
                wt[2 * p + hh, rows, :nk] = weights
                gs[2 * p + hh, rows, :nk] = grad.astype(BF16) * ok
                out = dot(weights, v[:nk]) * lanes
                total = out if total is None else total + out
            att[rows, pl.ds(off, 128)] = total


def attention_grad(act, slope, wt, gs, da, dpre):
    @pl.loop(0, HEADS // 2)
    def _(p):
        off = pl.multiple_of(128 * p, 128)
        vcols = pl.ds(512 + off, 128)
        qcols = pl.ds(1024 + off, 128)
        kcols = pl.ds(1536 + off, 128)
        v = act[:, vcols]
        q = act[:, qcols]
        k = act[:, kcols]
        d = da[:, pl.ds(off, 128)]
        qt = jnp.transpose(q)
        dt = jnp.transpose(d)
        dvs, dks = [], []
        dq = [None, None]
        for hh in range(2):
            lanes = half_lanes(hh)
            half = slice(64 * hh, 64 * hh + 64)
            dv, dk = [], []
            for t in range(2):
                rows = slice(256 * t, 256 * t + 256)
                nk = 256 * (t + 1)
                dm = d[rows] * lanes.astype(BF16)
                dw = dot_nt(dm, v[:nk])
                ds = (dw * gs[2 * p + hh, rows, :nk].astype(F32)).astype(BF16)
                part = dot(ds, k[:nk]) * lanes
                dq[t] = part if dq[t] is None else dq[t] + part
                dk.append(dot(qt[half, rows], ds))
                dv.append(dot(dt[half, rows], wt[2 * p + hh, rows, :nk]))
            dks.append(jnp.concatenate([dk[0] + dk[1][:, :256], dk[1][:, 256:]], axis=1))
            dvs.append(jnp.concatenate([dv[0] + dv[1][:, :256], dv[1][:, 256:]], axis=1))
        for t in range(2):
            rows = slice(256 * t, 256 * t + 256)
            dpre[rows, qcols] = dq[t].astype(BF16) * slope[rows, qcols]
        dk = jnp.transpose(jnp.concatenate(dks, axis=0))
        dv = jnp.transpose(jnp.concatenate(dvs, axis=0))
        dpre[:, kcols] = dk.astype(BF16) * slope[:, kcols]
        dpre[:, vcols] = dv.astype(BF16) * slope[:, vcols]


def gate_grad(att, act, slope, dy, wo, da, dpre, gated):
    for t in range(2):
        rows = slice(256 * t, 256 * t + 256)
        normed, scale = centred(att[rows])
        u = act[rows, :N].astype(F32)
        gated[rows] = (normed * u).astype(BF16)
        dg = dot_nt(dy[rows], wo[...]).astype(BF16).astype(F32)
        dpre[rows, :N] = (dg * normed).astype(BF16) * slope[rows, :N]
        da[rows] = norm_grad(dg * u, normed, scale).astype(BF16)


def out_grad(dy, gated, g):
    term = dot(jnp.transpose(dy[...]), gated[...]).astype(BF16)
    term = term.reshape(CHIPS, 2, 16, N)
    for c in range(2):
        for y in range(4):
            g[c, y, :, 64:80, :] = term[:, c, :, 128 * y : 128 * y + 128]


def in_grad(xht, dpre, g):
    @pl.loop(0, 8)
    def _(j):
        cols = pl.ds(pl.multiple_of(256 * j, 256), 256)
        term = dot(xht[...], dpre[:, cols]).astype(BF16)
        for half in range(2):
            for c in range(2):
                for y in range(4):
                    first = 256 * c + 64 * y
                    g[c, y, 2 * j + half, 0:64, :] = term[
                        first : first + 64, 128 * half : 128 * half + 128
                    ]


def row_grad(x, dy, dpre, w, dx):
    for t in range(2):
        rows = slice(256 * t, 256 * t + 256)
        dxh = dot_nt(dpre[rows], w[...]).astype(BF16).astype(F32)
        normed, scale = centred(x[rows].astype(F32))
        dx[rows] = (norm_grad(dxh, normed, scale) + dy[rows].astype(F32)).astype(BF16)


def spread(pos, dx, out):
    column = column_of(pos, SLOTS)
    for chunk in range(4):
        part = column[256 * chunk : 256 * chunk + 256]
        hot = jnp.concatenate(
            [onehot((iota((256, 128), 1) + 128 * b).astype(F32) == part) for b in range(4)],
            axis=1,
        )
        out[8 * chunk : 8 * chunk + 8] = dot(hot, dx[...]).astype(BF16).reshape(8, CAP, N)


def layer_kernel(
    rx, ry, ct, users, w, wo, dxp, g, x, dy, xh, xht, act, slope, mask, wt, gs, att, da, dpre, gated, dx
):
    pos = slot_positions(ct)
    compact(pos, rx, x)
    xh[...] = centred(x[...].astype(F32))[0].astype(BF16)
    xht[...] = jnp.transpose(xh[...])
    projection(xh, w, act, slope)
    allowed_mask(users, mask)
    attention(act, mask, wt, gs, att)
    compact(pos, ry, dy)
    gate_grad(att, act, slope, dy, wo, da, dpre, gated)
    out_grad(dy, gated, g)
    attention_grad(act, slope, wt, gs, da, dpre)
    in_grad(xht, dpre, g)
    row_grad(x, dy, dpre, w, dx)
    spread(pos, dx, dxp)


LAYER_SCRATCH = [
    pltpu.VMEM((N, N), BF16),
    pltpu.VMEM((N, N), BF16),
    pltpu.VMEM((N, N), BF16),
    pltpu.VMEM((N, N), BF16),
    pltpu.VMEM((N, 4 * N), BF16),
    pltpu.VMEM((N, 4 * N), BF16),
    pltpu.VMEM((N, N), BF16),
    pltpu.VMEM((HEADS, N, N), BF16),
    pltpu.VMEM((HEADS, N, N), BF16),
    pltpu.VMEM((N, N), F32),
    pltpu.VMEM((N, N), BF16),
    pltpu.VMEM((N, 4 * N), BF16),
    pltpu.VMEM((N, N), BF16),
    pltpu.VMEM((N, N), BF16),
]


def collect_kernel(
    dxp, g, place, ge, gw, gout,
    ret, r1, s1, r2, s2, r3, s3, r4, hot,
    bs, br, s1s, s1r, s2s, s2r, s3s, s3r, s4s, s4r, loc,
):
    me, rep = position()
    core = lax.rem(me, 2)
    chip = me // 2
    partner = chip * 2 + (1 - core)
    barrier = pltpu.get_barrier_semaphore()
    group_signal(barrier, me, rep)
    for i in range(1, REP):
        for c in range(2):
            pl.semaphore_signal(
                barrier, 1, device_id=(chip * 2 + c, lax.rem(rep + i, REP)), device_id_type=MESH
            )
    column = column_of(place[...].astype(F32), N)
    for b in range(8):
        hot[:, 128 * b : 128 * b + 128] = onehot(
            (iota((N, 128), 1) + 128 * b).astype(F32) == column
        )
    pl.semaphore_wait(barrier, DP - 1 + 2 * (REP - 1))

    def first(i):
        y = lax.rem(rep + i, REP)
        return y, remote(g.at[1 - core, y], r1.at[y], s1s.at[i], s1r.at[i], partner, rep)

    for i in (2, 1, 3, 0):
        first(i)[1].start()
    send_blocks(dxp, ret, bs, br, loc, me, rep)

    def second(i):
        y = lax.rem(rep + i, REP)
        return remote(s1.at[y], r2.at[i], s2s.at[i], s2r.at[i], me, y)

    for i in (2, 1, 3, 0):
        y, copy = first(i)
        copy.wait()
        s1[y] = (g[core, y].astype(F32) + r1[y].astype(F32)).astype(BF16)
        if i:
            second(i).start()
    for i in (2, 1, 3):
        second(i).wait()
    s2[...] = (
        s1[rep].astype(F32) + r2[1].astype(F32) + r2[2].astype(F32) + r2[3].astype(F32)
    ).astype(BF16)

    def third(i, mine):
        other = lax.rem(chip + i, CHIPS)
        place_in = chip if mine else other
        return remote(
            s2.at[other], r3.at[place_in], s3s.at[other], s3r.at[place_in], other * 2 + core, rep
        )

    @pl.loop(1, CHIPS)
    def _(i):
        third(i, True).start()

    @pl.loop(1, CHIPS)
    def _(i):
        third(i, False).wait()

    r3[chip] = s2[chip]
    total = r3[0].astype(F32)
    for i in range(1, CHIPS):
        total = total + r3[i].astype(F32)
    s3[...] = total.astype(BF16)

    def fourth(i, c, mine):
        y = lax.rem(rep + i, REP)
        other = c if c is not None else core
        to = chip * 2 + (1 - core if c else core)
        from_y, from_c = (rep, core) if mine else (y, 1 - core if c else core)
        slot = from_y * 2 + from_c
        to_slot = y * 2 + (1 - core if c else core)
        del other
        return remote(s3, r4.at[slot], s4s.at[to_slot], s4r.at[slot], to, y)

    for i in range(REP):
        for c in (0, 1):
            if i or c:
                fourth(i, c, True).start()
    r4[rep * 2 + core] = s3[...]
    for i in range(REP):
        for c in (0, 1):
            if i or c:
                fourth(i, c, False).wait()
    for y in range(4):
        for c in range(2):
            block = r4[y * 2 + c, 0:64, :].astype(F32)
            block = jnp.where(core == 1, pltpu.roll(block, 64, 1), block)
            gw[256 * c + 64 * y : 256 * c + 64 * y + 64, :] = block[:, :64]
        tail = r4[y * 2 + core, 64:80, :].astype(F32)
        tail = jnp.concatenate([tail, jnp.zeros((112, 128), F32)], axis=0)
        gout[128 * y : 128 * y + 128, :] = jnp.transpose(tail)[:, :16]
    wait_blocks(dxp, ret, bs, br, loc, me, rep)
    rows = ret[...].reshape(SLOTS, N)
    ge[...] = dot(hot[...], rows).astype(BF16)


DMA = pltpu.SemaphoreType.DMA
COLLECT_SCRATCH = [
    pltpu.VMEM((DP, CAP, N), BF16),
    pltpu.VMEM((4, CHIPS, 80, 128), BF16),
    pltpu.VMEM((4, CHIPS, 80, 128), BF16),
    pltpu.VMEM((4, CHIPS, 80, 128), BF16),
    pltpu.VMEM((CHIPS, 80, 128), BF16),
    pltpu.VMEM((CHIPS, 80, 128), BF16),
    pltpu.VMEM((80, 128), BF16),
    pltpu.VMEM((8, 80, 128), BF16),
    pltpu.VMEM((N, SLOTS), BF16),
    DMA((DP,)), DMA((DP,)), DMA((4,)), DMA((4,)), DMA((4,)), DMA((4,)),
    DMA((CHIPS,)), DMA((CHIPS,)), DMA((8,)), DMA((8,)), DMA,
]

BUFFER = jax.ShapeDtypeStruct((DP, CAP, N), BF16)
VM = pl.BlockSpec(memory_space=pltpu.VMEM)


def on_device(events, grad_out, w_uvqk, w_out, send_place, send_counts, user_ids):
    rx, ry, ct = pl.pallas_call(
        dispatch_kernel,
        name="dispatch",
        out_shape=(BUFFER, BUFFER, jax.ShapeDtypeStruct((DP, 1, DP), I32)),
        in_specs=[VM] * 4,
        out_specs=(VM,) * 3,
        scratch_shapes=[
            pltpu.VMEM((DP, CAP, N), BF16), pltpu.VMEM((DP, CAP, N), BF16),
            DMA((DP,)), DMA((DP,)), DMA((DP,)), DMA((DP,)), DMA((DP,)), DMA((DP,)), DMA((3,)),
        ],
        compiler_params=pltpu.CompilerParams(
            collective_id=0, has_side_effects=True, vmem_limit_bytes=VMEM_LIMIT
        ),
    )(events, grad_out, send_place, send_counts)
    dxp, g = pl.pallas_call(
        layer_kernel,
        name="layer",
        out_shape=(BUFFER, jax.ShapeDtypeStruct((2, 4, CHIPS, 80, 128), BF16)),
        in_specs=[VM] * 6,
        out_specs=(VM,) * 2,
        scratch_shapes=LAYER_SCRATCH,
        compiler_params=pltpu.CompilerParams(vmem_limit_bytes=VMEM_LIMIT),
    )(rx, ry, ct, user_ids, w_uvqk, w_out)
    ge, gw, gout = pl.pallas_call(
        collect_kernel,
        name="collect",
        out_shape=(
            jax.ShapeDtypeStruct((N, N), BF16),
            jax.ShapeDtypeStruct((N, 64), F32),
            jax.ShapeDtypeStruct((N, 16), F32),
        ),
        in_specs=[VM] * 3,
        out_specs=(VM,) * 3,
        scratch_shapes=COLLECT_SCRATCH,
        compiler_params=pltpu.CompilerParams(
            collective_id=1, has_side_effects=True, vmem_limit_bytes=VMEM_LIMIT
        ),
    )(dxp, g, send_place)
    return ge, gw, gout


def solution(mesh):
    rows = P(("dp", "rep"), None)
    return jax.shard_map(
        on_device,
        mesh=mesh,
        in_specs=(rows, rows, P(), P(), rows, rows, rows),
        out_specs=(rows, P(None, "dp"), P(None, "dp")),
        check_vma=False,
    )
```

```python
import jax
import jax.numpy as jnp
from jax import lax
from jax.experimental import pallas as pl
from jax.experimental.pallas import tpu as pltpu
from jax.sharding import PartitionSpec as P

HEADS = 8
EPSILON = 1e-05
F32 = jnp.float32
BF16 = jnp.bfloat16
I32 = jnp.int32
MESH = pl.DeviceIdType.MESH
N = 512
DP = 32
REP = 4
CAP = 32
SLOTS = 1024
CHIPS = 16
VMEM_LIMIT = 62 * 1024 * 1024


def dot(a, b):
    return jnp.dot(a, b, preferred_element_type=F32)


def dot_nt(a, b):
    return lax.dot_general(a, b, (((1,), (1,)), ((), ())), preferred_element_type=F32)


def iota(shape, dim):
    return lax.broadcasted_iota(I32, shape, dim)


def onehot(mask):
    return jnp.where(mask, 1.0, 0.0).astype(BF16)


def column_of(row, width):
    return jnp.transpose(jnp.broadcast_to(row, (128, width)))


def remote(src, dst, send, recv, dp, rep):
    return pltpu.make_async_remote_copy(
        src_ref=src,
        dst_ref=dst,
        send_sem=send,
        recv_sem=recv,
        device_id=(dp, rep),
        device_id_type=MESH,
    )


def signal(barrier, dp, rep):
    pl.semaphore_signal(barrier, 1, device_id=(dp, rep), device_id_type=MESH)


class Place:
    def __init__(self):
        self.me = lax.axis_index("dp")
        self.rep = lax.axis_index("rep")
        self.core = lax.rem(self.me, 2)
        self.chip = self.me // 2
        self.x = self.me // 8
        self.z = lax.rem(self.chip, 4)
        self.partner = self.chip * 2 + (1 - self.core)


def pack(place, rows, out):
    for chunk in range(4):
        hot = onehot(iota((256, N), 0) + 256 * chunk == place)
        out[8 * chunk : 8 * chunk + 8] = dot(hot, rows).astype(BF16).reshape(8, CAP, N)


def each_peer(at, dx, body):
    column = lax.rem(at.x + dx, 4) * 8
    inner = lax.rem(at.me, 8)

    @pl.loop(0 if dx else 1, 8)
    def _(j):
        body(column + lax.rem(inner + j, 8))


class Exchange:
    def __init__(self, at, src, dst, send, recv, local, whole=False):
        self.at, self.src, self.dst = at, src, dst
        self.sems, self.local, self.whole = (send, recv), local, whole

    def block(self, peer):
        return self.src if self.whole else self.src.at[peer]

    def own(self):
        me = self.at.me
        return pltpu.make_async_copy(self.block(me), self.dst.at[me], self.local)

    def start(self, dx):
        at, (send, recv) = self.at, self.sems

        def body(peer):
            remote(
                self.block(peer), self.dst.at[at.me], send.at[peer], recv.at[at.me], peer, at.rep
            ).start()

        each_peer(at, dx, body)
        if dx == 0:
            self.own().start()

    def start_all(self):
        for dx in (2, 1, 3, 0):
            self.start(dx)

    def wait(self):
        at, (send, recv) = self.at, self.sems

        def body(peer):
            remote(
                self.block(peer), self.dst.at[peer], send.at[peer], recv.at[peer], peer, at.rep
            ).wait()

        for dx in (0, 1, 3, 2):
            each_peer(at, dx, body)
        self.own().wait()


class Reduce:
    def __init__(self, at, g, r1, s1, r2, s2, r3, r3w, s3, r4, sems):
        self.at = at
        self.g, self.r1, self.s1, self.r2, self.s2 = g, r1, s1, r2, s2
        self.r3, self.r3w, self.s3, self.r4 = r3, r3w, s3, r4
        (self.a_s, self.a_r, self.b_s, self.b_r, self.c_s, self.c_r,
         self.w_s, self.w_r, self.d_s, self.d_r) = sems

    def pair(self, s):
        at = self.at
        return remote(
            self.g.at[1 - at.core, s], self.r1.at[s], self.a_s.at[s], self.a_r.at[s], at.partner, at.rep
        )

    def over_y(self, s, i):
        at = self.at
        y = lax.rem(at.rep + i, REP)
        return remote(
            self.s1.at[s, y], self.r2.at[s, i], self.b_s.at[s, i], self.b_r.at[s, i], at.me, y
        )

    def pair_done(self, s):
        at = self.at
        self.pair(s).wait()
        self.s1[s] = (self.g[at.core, s].astype(F32) + self.r1[s].astype(F32)).astype(BF16)
        for i in (2, 1, 3):
            self.over_y(s, i).start()

    def y_done(self, s):
        for i in (2, 1, 3):
            self.over_y(s, i).wait()
        total = self.s1[s, self.at.rep].astype(F32)
        for i in (1, 2, 3):
            total = total + self.r2[s, i].astype(F32)
        self.s2[s] = total.astype(BF16)

    def column(self, p, x, slot):
        at = self.at
        to = x * 4 + p
        return remote(
            self.s2.at[1 + p, pl.ds(64 * x, 64)], self.r3.at[slot],
            self.c_s.at[p, x], self.c_r.at[slot], to * 2 + at.core, at.rep,
        )

    def columns_start(self, p):
        at = self.at
        for x in range(4):

            @pl.when(x * 4 + p != at.chip)
            def _():
                self.column(p, x, at.chip).start()

    def out_rows(self, other, slot):
        at = self.at
        return remote(
            self.s2.at[0, pl.ds(pl.multiple_of(16 * other, 16), 16)], self.r3w.at[slot],
            self.w_s.at[other], self.w_r.at[slot], other * 2 + at.core, at.rep,
        )

    def out_start(self):
        @pl.loop(1, CHIPS)
        def _(i):
            self.out_rows(lax.rem(self.at.chip + i, CHIPS), self.at.chip).start()

    def gather(self, i, other_core, mine):
        at = self.at
        y = lax.rem(at.rep + i, REP)
        core = 1 - at.core if other_core else at.core
        slot = at.rep * 2 + at.core if mine else y * 2 + core
        return remote(
            self.s3, self.r4.at[slot], self.d_s.at[y * 2 + core], self.d_r.at[slot], at.chip * 2 + core, y
        )

    def finish(self):
        at = self.at

        @pl.loop(1, CHIPS)
        def _(i):
            other = lax.rem(at.chip + i, CHIPS)
            self.out_rows(other, other).wait()
            remote(
                self.r3.at[other], self.r3.at[other], self.d_s.at[0], self.c_r.at[other], other * 2 + at.core, at.rep
            ).wait_recv()

        for p in range(4):
            for x in range(4):

                @pl.when(x * 4 + p != at.chip)
                def _(p=p, x=x):
                    self.column(p, x, at.chip).wait_send()

        self.r3[at.chip] = self.s2[1 + at.z, pl.ds(pl.multiple_of(64 * at.x, 64), 64)]
        self.r3w[at.chip] = self.s2[0, pl.ds(pl.multiple_of(16 * at.chip, 16), 16)]
        for ref, rows in ((self.r3, slice(0, 64)), (self.r3w, slice(64, 80))):
            total = ref[0].astype(F32)
            for i in range(1, CHIPS):
                total = total + ref[i].astype(F32)
            self.s3[rows] = total.astype(BF16)
        order = [(i, other) for i in (2, 1, 3, 0) for other in (True, False) if i or other]
        for i, other in order:
            self.gather(i, other, True).start()
        self.r4[at.rep * 2 + at.core] = self.s3[...]
        for i, other in order:
            self.gather(i, other, False).wait()


def slot_positions(ct):
    me = lax.axis_index("dp")
    table = ct[:, 0, :]
    mine = jnp.where(iota((DP, DP), 1) == me, table, 0).astype(F32)
    counts = jnp.sum(mine, axis=1, keepdims=True)
    source = iota((DP, SLOTS), 0)
    slot_source = iota((DP, SLOTS), 1) // CAP
    start = jnp.sum(jnp.where(source < slot_source, counts, 0.0), axis=0, keepdims=True)
    count = jnp.sum(jnp.where(source == slot_source, counts, 0.0), axis=0, keepdims=True)
    within = lax.rem(iota((1, SLOTS), 1), CAP).astype(F32)
    return jnp.where(within < count, start + within, -1.0)


def compact(pos, rows_ref, out_ref):
    rows = rows_ref[...].reshape(SLOTS, N)
    for chunk in range(2):
        index = (iota((256, SLOTS), 0) + 256 * chunk).astype(F32)
        hot = onehot(index == pos)
        out_ref[256 * chunk : 256 * chunk + 256] = dot(hot, rows).astype(BF16)


def centred(values):
    center = values - jnp.mean(values, axis=-1, keepdims=True)
    spread = jnp.mean(center * center, axis=-1, keepdims=True)
    scale = lax.rsqrt(spread + EPSILON)
    return center * scale, scale


def norm_grad(grad, normed, scale):
    lead = jnp.mean(grad, axis=-1, keepdims=True)
    along = jnp.mean(grad * normed, axis=-1, keepdims=True)
    return scale * (grad - lead - normed * along)


def sigmoid(x):
    return 0.5 * jnp.tanh(0.5 * x) + 0.5


def allowed_mask(users, mask):
    row = users[...].astype(F32)
    column = column_of(row, N)
    for b in range(4):
        keys = slice(128 * b, 128 * b + 128)
        same = column == row[:, keys]
        causal = iota((N, 128), 1) + 128 * b <= iota((N, 128), 0)
        mask[:, keys] = onehot(same & causal)


def half_lanes(hh):
    return jnp.where(iota((1, 128), 1) // 64 == hh, 1.0, 0.0)


U, V, Q, K = (slice(128 * i, 128 * i + 128) for i in range(4))


def pair_forward(p, xh, wp, mask, act, slope, wt, gs, att):
    for half in range(2):
        cols = slice(256 * half, 256 * half + 256)
        pre = dot(xh[...], wp[p, :, cols])
        sig = sigmoid(pre)
        silu = pre * sig
        act[p, :, cols] = silu.astype(BF16)
        slope[p, :, cols] = (sig + silu * (1.0 - sig)).astype(BF16)
    v, q, k = act[p, :, V], act[p, :, Q], act[p, :, K]
    for t in range(2):
        rows = slice(256 * t, 256 * t + 256)
        nk = 256 * (t + 1)
        total = None
        for hh in range(2):
            lanes = half_lanes(hh)
            qm = q[rows] * lanes.astype(BF16)
            half = dot_nt(qm, k[:nk]) * 0.0625
            th = jnp.tanh(half)
            silu = half + half * th
            sig = 0.5 + 0.5 * th
            grad = (sig + silu * (1.0 - sig)) * 0.125
            ok = mask[rows, :nk]
            weights = silu.astype(BF16) * ok
            wt[2 * p + hh, rows, :nk] = weights
            gs[2 * p + hh, rows, :nk] = grad.astype(BF16) * ok
            out = dot(weights, v[:nk]) * lanes
            total = out if total is None else total + out
        att[rows, pl.ds(pl.multiple_of(128 * p, 128), 128)] = total


def pair_backward(p, act, slope, wt, gs, da, dpre):
    v, q, k = act[p, :, V], act[p, :, Q], act[p, :, K]
    d = da[:, pl.ds(pl.multiple_of(128 * p, 128), 128)]
    qt = jnp.transpose(q)
    dt = jnp.transpose(d)
    dvs, dks = [], []
    dq = [None, None]
    for hh in range(2):
        lanes = half_lanes(hh)
        half = slice(64 * hh, 64 * hh + 64)
        dv, dk = [], []
        for t in range(2):
            rows = slice(256 * t, 256 * t + 256)
            nk = 256 * (t + 1)
            dm = d[rows] * lanes.astype(BF16)
            dw = dot_nt(dm, v[:nk])
            ds = (dw * gs[2 * p + hh, rows, :nk].astype(F32)).astype(BF16)
            part = dot(ds, k[:nk]) * lanes
            dq[t] = part if dq[t] is None else dq[t] + part
            dk.append(dot(qt[half, rows], ds))
            dv.append(dot(dt[half, rows], wt[2 * p + hh, rows, :nk]))
        dks.append(jnp.concatenate([dk[0] + dk[1][:, :256], dk[1][:, 256:]], axis=1))
        dvs.append(jnp.concatenate([dv[0] + dv[1][:, :256], dv[1][:, 256:]], axis=1))
    for t in range(2):
        rows = slice(256 * t, 256 * t + 256)
        dpre[p, rows, Q] = dq[t].astype(BF16) * slope[p, rows, Q]
    dk = jnp.transpose(jnp.concatenate(dks, axis=0))
    dv = jnp.transpose(jnp.concatenate(dvs, axis=0))
    dpre[p, :, K] = dk.astype(BF16) * slope[p, :, K]
    dpre[p, :, V] = dv.astype(BF16) * slope[p, :, V]


def gate_grad(att, act, slope, dy, wo, da, dpre, gated):
    for t in range(2):
        rows = slice(256 * t, 256 * t + 256)
        normed, scale = centred(att[rows])
        u = jnp.concatenate([act[p, rows, U] for p in range(4)], axis=1).astype(F32)
        gated[rows] = (normed * u).astype(BF16)
        dg = dot_nt(dy[rows], wo[...]).astype(BF16).astype(F32)
        du = (dg * normed).astype(BF16)
        for p in range(4):
            dpre[p, rows, U] = du[:, 128 * p : 128 * p + 128] * slope[p, rows, U]
        da[rows] = norm_grad(dg * u, normed, scale).astype(BF16)


def out_grad(dy, gated, g):
    term = dot(jnp.transpose(dy[...]), gated[...]).astype(BF16)
    term = term.reshape(CHIPS, 2, 16, N)
    for c in range(2):
        for y in range(4):
            g[c, 0, y] = term[:, c, :, 128 * y : 128 * y + 128].reshape(256, 128)


def pair_in_grad(p, xht, dpre, g):
    for half in range(2):
        term = dot(xht[...], dpre[p, :, 256 * half : 256 * half + 256]).astype(BF16)
        for x in range(2):
            for c in range(2):
                for y in range(4):
                    first = 256 * c + 64 * y
                    row = 64 * (2 * half + x)
                    g[c, 1 + p, y, row : row + 64, :] = term[
                        first : first + 64, 128 * x : 128 * x + 128
                    ]


def row_grad(x, dy, dpre, wp, dx):
    for t in range(2):
        rows = slice(256 * t, 256 * t + 256)
        dxh = dot_nt(dpre[0, rows], wp[0])
        for p in range(1, 4):
            dxh = dxh + dot_nt(dpre[p, rows], wp[p])
        dxh = dxh.astype(BF16).astype(F32)
        normed, scale = centred(x[rows].astype(F32))
        dx[rows] = (norm_grad(dxh, normed, scale) + dy[rows].astype(F32)).astype(BF16)


def spread(chunk, column, dx, out):
    part = column[pl.ds(pl.multiple_of(256 * chunk, 256), 256)]
    hot = jnp.concatenate(
        [onehot((iota((256, 128), 1) + 128 * b).astype(F32) == part) for b in range(4)], axis=1
    )
    out[pl.ds(8 * chunk, 8)] = dot(hot, dx[...]).astype(BF16).reshape(8, CAP, N)


def layer_kernel(
    ev_any, go_any, w_any, wo_any, place, cnt, users,
    ret, r4,
    ev, go, wp, wo, sx, sy, rx, ry, ct, dxp,
    x, dy, xh, xht, act, slope, mask, wt, gs, att, da, dpre, gated, dx, column,
    g, r1, s1, r2, s2, r3, r3w, s3,
    xs, xr, ys, yr, cs, cr, bs, br, loc, load,
    a_s, a_r, b_s, b_r, c_s, c_r, w_s, w_r, d_s, d_r,
):
    at = Place()
    barrier = pltpu.get_barrier_semaphore()
    for dxo in range(4):
        each_peer(at, dxo, lambda peer: signal(barrier, peer, at.rep))
    for i in range(1, REP):
        for c in range(2):
            signal(barrier, at.chip * 2 + c, lax.rem(at.rep + i, REP))
    loads = [pltpu.make_async_copy(ev_any, ev, load.at[0]), pltpu.make_async_copy(go_any, go, load.at[1])]
    for p in range(4):
        for i in range(4):
            loads.append(
                pltpu.make_async_copy(
                    w_any.at[:, pl.ds(512 * i + 128 * p, 128)],
                    wp.at[p, :, pl.ds(128 * i, 128)],
                    load.at[2 + 4 * p + i],
                )
            )
    loads.append(pltpu.make_async_copy(wo_any, wo, load.at[18]))
    for copy in loads:
        copy.start()
    loads[0].wait()
    pack(place[...], ev[...], sx)
    to_x = Exchange(at, sx, rx, xs, xr, loc.at[0])
    to_y = Exchange(at, sy, ry, ys, yr, loc.at[1])
    counts = Exchange(at, cnt, ct, cs, cr, loc.at[2], whole=True)
    back = Exchange(at, dxp, ret, bs, br, loc.at[3])
    reduce = Reduce(
        at, g, r1, s1, r2, s2, r3, r3w, s3, r4,
        (a_s, a_r, b_s, b_r, c_s, c_r, w_s, w_r, d_s, d_r),
    )
    pl.semaphore_wait(barrier, DP - 1 + 2 * (REP - 1))
    counts.start_all()
    to_x.start_all()
    loads[1].wait()
    pack(place[...], go[...], sy)
    to_y.start_all()
    allowed_mask(users, mask)
    counts.wait()
    pos = slot_positions(ct)
    column[...] = column_of(pos, SLOTS)
    for copy in loads[2:]:
        copy.wait()
    to_x.wait()
    compact(pos, rx, x)
    xh[...] = centred(x[...].astype(F32))[0].astype(BF16)
    xht[...] = jnp.transpose(xh[...])

    @pl.loop(0, 4)
    def _(p):
        pair_forward(p, xh, wp, mask, act, slope, wt, gs, att)

    to_y.wait()
    compact(pos, ry, dy)
    gate_grad(att, act, slope, dy, wo, da, dpre, gated)
    out_grad(dy, gated, g)
    reduce.pair(0).start()

    @pl.loop(0, 4)
    def _(p):
        pair_backward(p, act, slope, wt, gs, da, dpre)
        pair_in_grad(p, xht, dpre, g)
        reduce.pair(1 + p).start()
        reduce.pair_done(p)

        @pl.when(p >= 1)
        def _():
            reduce.y_done(p - 1)

    reduce.out_start()
    for p in range(2):
        reduce.columns_start(p)
    row_grad(x, dy, dpre, wp, dx)
    reduce.pair_done(4)
    reduce.y_done(3)
    reduce.columns_start(2)
    for dxo in (2, 1, 3):
        spread(lax.rem(at.x + dxo, 4), column, dx, dxp)
        back.start(dxo)
    spread(at.x, column, dx, dxp)
    reduce.y_done(4)
    reduce.columns_start(3)
    back.start(0)
    reduce.finish()
    back.wait()


def finish_kernel(ret, r4, place, ge, gw, gout):
    core = lax.rem(lax.axis_index("dp"), 2)
    column = column_of(place[...].astype(F32), N)
    hot = jnp.concatenate(
        [onehot((iota((N, 128), 1) + 128 * b).astype(F32) == column) for b in range(8)], axis=1
    )
    ge[...] = dot(hot, ret[...].reshape(SLOTS, N)).astype(BF16)
    for c in range(2):
        for half in range(2):
            block = jnp.concatenate([r4[4 * half + c, :64], r4[4 * half + 2 + c, :64]], axis=0)
            block = jnp.transpose(block.astype(F32))
            first = 256 * c + 128 * half
            gw[:, first : first + 128] = jnp.where(core == 1, block[64:], block[:64])
    for y in range(4):
        gout[:, 128 * y : 128 * y + 128] = r4[2 * y + core, 64:80].astype(F32)


DMA = pltpu.SemaphoreType.DMA
BLOCKS = pltpu.VMEM((DP, CAP, N), BF16)
SQUARE = pltpu.VMEM((N, N), BF16)
PAIRS = pltpu.VMEM((4, N, N), BF16)
TERMS = pltpu.VMEM((5, 4, 256, 128), BF16)
SCRATCH = [
    SQUARE, SQUARE, PAIRS, SQUARE,
    BLOCKS, BLOCKS, BLOCKS, BLOCKS, pltpu.VMEM((DP, 1, DP), I32), BLOCKS,
    SQUARE, SQUARE, SQUARE, SQUARE, PAIRS, PAIRS, SQUARE,
    pltpu.VMEM((HEADS, N, N), BF16), pltpu.VMEM((HEADS, N, N), BF16),
    pltpu.VMEM((N, N), F32), SQUARE, PAIRS, SQUARE, SQUARE,
    pltpu.VMEM((SLOTS, 128), F32),
    pltpu.VMEM((2, 5, 4, 256, 128), BF16), TERMS, TERMS, TERMS,
    pltpu.VMEM((5, 256, 128), BF16),
    pltpu.VMEM((CHIPS, 64, 128), BF16), pltpu.VMEM((CHIPS, 16, 128), BF16),
    pltpu.VMEM((80, 128), BF16),
    DMA((DP,)), DMA((DP,)), DMA((DP,)), DMA((DP,)), DMA((DP,)), DMA((DP,)), DMA((DP,)), DMA((DP,)),
    DMA((4,)), DMA((19,)),
    DMA((5,)), DMA((5,)), DMA((5, 4)), DMA((5, 4)), DMA((4, 4)), DMA((CHIPS,)),
    DMA((CHIPS,)), DMA((CHIPS,)), DMA((8,)), DMA((8,)),
]
VM = pl.BlockSpec(memory_space=pltpu.VMEM)
ANY = pl.BlockSpec(memory_space=pl.ANY)


def on_device(events, grad_out, w_uvqk, w_out, send_place, send_counts, user_ids):
    ret, r4 = pl.pallas_call(
        layer_kernel,
        name="layer",
        out_shape=(
            jax.ShapeDtypeStruct((DP, CAP, N), BF16),
            jax.ShapeDtypeStruct((8, 80, 128), BF16),
        ),
        in_specs=[ANY] * 4 + [VM] * 3,
        out_specs=(VM,) * 2,
        scratch_shapes=SCRATCH,
        compiler_params=pltpu.CompilerParams(
            collective_id=0, has_side_effects=True, vmem_limit_bytes=VMEM_LIMIT
        ),
    )(events, grad_out, w_uvqk, w_out, send_place, send_counts, user_ids)
    ge, gw, gout = pl.pallas_call(
        finish_kernel,
        name="finish",
        out_shape=(
            jax.ShapeDtypeStruct((N, N), BF16),
            jax.ShapeDtypeStruct((64, N), F32),
            jax.ShapeDtypeStruct((16, N), F32),
        ),
        in_specs=[VM] * 3,
        out_specs=(VM,) * 3,
        compiler_params=pltpu.CompilerParams(vmem_limit_bytes=32 * 1024 * 1024),
    )(ret, r4, send_place)
    return ge, gw.T, gout.T


def solution(mesh):
    rows = P(("dp", "rep"), None)
    return jax.shard_map(
        on_device,
        mesh=mesh,
        in_specs=(rows, rows, P(), P(), rows, rows, rows),
        out_specs=(rows, P(None, "dp"), P(None, "dp")),
        check_vma=False,
    )
```

```python
import jax
import jax.numpy as jnp
from jax import lax
from jax.experimental import pallas as pl
from jax.experimental.pallas import tpu as pltpu
from jax.sharding import PartitionSpec as P

HEADS = 8
EPSILON = 1e-05
F32 = jnp.float32
BF16 = jnp.bfloat16
I32 = jnp.int32
MESH = pl.DeviceIdType.MESH
N = 512
DP = 32
REP = 4
CAP = 32
SLOTS = 1024
CHIPS = 16
VMEM_LIMIT = 62 * 1024 * 1024


def dot(a, b):
    return jnp.dot(a, b, preferred_element_type=F32)


def dot_nt(a, b):
    return lax.dot_general(a, b, (((1,), (1,)), ((), ())), preferred_element_type=F32)


def iota(shape, dim):
    return lax.broadcasted_iota(I32, shape, dim)


def onehot(mask):
    return jnp.where(mask, 1.0, 0.0).astype(BF16)


def column_of(row, width):
    return jnp.transpose(jnp.broadcast_to(row, (128, width)))


def remote(src, dst, send, recv, dp, rep):
    return pltpu.make_async_remote_copy(
        src_ref=src,
        dst_ref=dst,
        send_sem=send,
        recv_sem=recv,
        device_id=(dp, rep),
        device_id_type=MESH,
    )


def signal(barrier, dp, rep):
    pl.semaphore_signal(barrier, 1, device_id=(dp, rep), device_id_type=MESH)


class Place:
    def __init__(self):
        self.me = lax.axis_index("dp")
        self.rep = lax.axis_index("rep")
        self.core = lax.rem(self.me, 2)
        self.chip = self.me // 2
        self.x = self.me // 8
        self.z = lax.rem(self.chip, 4)
        self.partner = self.chip * 2 + (1 - self.core)


def pack(place, rows, out):
    for chunk in range(4):
        hot = onehot(iota((256, N), 0) + 256 * chunk == place)
        out[8 * chunk : 8 * chunk + 8] = dot(hot, rows).astype(BF16).reshape(8, CAP, N)


def each_peer(at, dx, body):
    column = lax.rem(at.x + dx, 4) * 8
    inner = lax.rem(at.me, 8)

    @pl.loop(0 if dx else 1, 8)
    def _(j):
        body(column + lax.rem(inner + j, 8))


def drain(ref, sem):
    pltpu.make_async_copy(ref, ref, sem).wait()


class Exchange:
    def __init__(self, at, src, dst, send, recv, whole=False):
        self.at, self.src, self.dst = at, src, dst
        self.send, self.recv, self.whole = send, recv, whole

    def block(self, peer):
        return self.src if self.whole else self.src.at[peer]

    def to(self, peer):
        at = self.at
        remote(self.block(peer), self.dst.at[at.me], self.send, self.recv, peer, at.rep).start()

    def own(self):
        me = self.at.me
        pltpu.make_async_copy(self.block(me), self.dst.at[me], self.recv).start()

    def start_all(self):
        for dx in (2, 1, 3, 0):
            each_peer(self.at, dx, self.to)
        self.own()

    def start(self, dx, steps):
        at = self.at
        column = lax.rem(at.x + dx, 4) * 8
        for j in steps:
            if dx == 0 and j == 0:
                self.own()
            else:
                self.to(column + lax.rem(lax.rem(at.me, 8) + j, 8))

    def wait(self):
        drain(self.dst, self.recv)
        drain(self.dst.at[pl.ds(0, DP - 1)], self.send)


class Reduce:
    def __init__(self, at, refs, sems):
        self.at = at
        (self.g, self.r1, self.s1, self.r2, self.s2, self.r2x, self.s2x, self.r2y, self.s3x,
         self.r3, self.r3z, self.r3w, self.s3, self.r4) = refs
        (self.a_s, self.a_r, self.b_s, self.b_r, self.x_s, self.x_r, self.y_s, self.y_r,
         self.z_s, self.z_r, self.c_s, self.c_r, self.w_s, self.w_r, self.d_s, self.d_r) = sems

    def pair(self, s):
        at = self.at
        return remote(
            self.g.at[1 - at.core, s], self.r1.at[s], self.a_s.at[s], self.a_r.at[s], at.partner, at.rep
        )

    def pair_done(self, s):
        at = self.at
        self.pair(s).wait()
        self.s1[s] = (self.g[at.core, s].astype(F32) + self.r1[s].astype(F32)).astype(BF16)
        for i in (2, 1, 3):
            if s in (1, 2):
                x = lax.rem(at.x + i, 4)
                remote(
                    self.s1.at[s, :, pl.ds(pl.multiple_of(64 * x, 64), 64)], self.r2x.at[s - 1, i],
                    self.x_s.at[s - 1], self.x_r.at[s - 1], x * 8 + lax.rem(at.me, 8), at.rep,
                ).start()
            else:
                y = lax.rem(at.rep + i, REP)
                remote(
                    self.s1.at[s, y], self.r2.at[s, i], self.b_s.at[s], self.b_r.at[s], at.me, y
                ).start()

    def y_done(self, s):
        drain(self.r2.at[s, pl.ds(1, 3)], self.b_r.at[s])
        drain(self.r2.at[s, pl.ds(1, 3)], self.b_s.at[s])
        total = self.s1[s, self.at.rep].astype(F32)
        for i in (1, 2, 3):
            total = total + self.r2[s, i].astype(F32)
        self.s2[s] = total.astype(BF16)

    def x_done(self, p):
        at = self.at
        drain(self.r2x.at[p, pl.ds(1, 3)], self.x_r.at[p])
        drain(self.r2x.at[p, pl.ds(1, 3)], self.x_s.at[p])
        total = self.s1[1 + p, :, pl.ds(pl.multiple_of(64 * at.x, 64), 64)].astype(F32)
        for i in (1, 2, 3):
            total = total + self.r2x[p, i].astype(F32)
        self.s2x[p] = total.astype(BF16)
        for i in (2, 1, 3):
            y = lax.rem(at.rep + i, REP)
            remote(
                self.s2x.at[p, y], self.r2y.at[p, i], self.y_s.at[p], self.y_r.at[p], at.me, y
            ).start()

    def xy_done(self, p):
        at = self.at
        drain(self.r2y.at[p, pl.ds(1, 3)], self.y_r.at[p])
        drain(self.r2y.at[p, pl.ds(1, 3)], self.y_s.at[p])
        total = self.s2x[p, at.rep].astype(F32)
        for i in (1, 2, 3):
            total = total + self.r2y[p, i].astype(F32)
        self.s3x[p] = total.astype(BF16)

        @pl.when(at.z != p)
        def _():
            to = at.x * 4 + p
            remote(
                self.s3x.at[p], self.r3z.at[at.z], self.z_s.at[p], self.z_r, to * 2 + at.core, at.rep
            ).start()

    def columns_start(self, p):
        at = self.at
        for x in (2, 1, 3, 0):
            to = x * 4 + p

            @pl.when(to != at.chip)
            def _(x=x, to=to):
                remote(
                    self.s2.at[1 + p, pl.ds(64 * x, 64)], self.r3.at[at.chip], self.c_s, self.c_r,
                    to * 2 + at.core, at.rep,
                ).start()

    def out_start(self):
        at = self.at

        @pl.loop(1, CHIPS)
        def _(i):
            other = lax.rem(at.chip + i, CHIPS)
            remote(
                self.s2.at[0, pl.ds(pl.multiple_of(16 * other, 16), 16)], self.r3w.at[at.chip],
                self.w_s, self.w_r, other * 2 + at.core, at.rep,
            ).start()

    def total(self, ref, count, rows):
        total = ref[0].astype(F32)
        for i in range(1, count):
            total = total + ref[i].astype(F32)
        self.s3[rows] = total.astype(BF16)

    def finish(self):
        at = self.at
        drain(self.r3w.at[pl.ds(0, CHIPS - 1)], self.w_r)
        drain(self.r3w.at[pl.ds(0, CHIPS - 1)], self.w_s)
        self.r3w[at.chip] = self.s2[0, pl.ds(pl.multiple_of(16 * at.chip, 16), 16)]
        self.total(self.r3w, CHIPS, slice(64, 80))

        @pl.when(at.z < 2)
        def _():
            drain(self.r3z.at[pl.ds(0, 3)], self.z_r)
            self.r3z[at.z] = self.s3x[at.z]
            self.total(self.r3z, 4, slice(0, 64))

        @pl.when(at.z >= 2)
        def _():
            drain(self.r3.at[pl.ds(0, CHIPS - 1)], self.c_r)
            self.r3[at.chip] = self.s2[1 + at.z, pl.ds(pl.multiple_of(64 * at.x, 64), 64)]
            self.total(self.r3, CHIPS, slice(0, 64))

        for i in (2, 1, 3, 0):
            for core in (1 - at.core, at.core):
                if i or core is not at.core:
                    y = lax.rem(at.rep + i, REP)
                    remote(
                        self.s3, self.r4.at[at.rep * 2 + at.core], self.d_s, self.d_r, at.chip * 2 + core, y
                    ).start()
        pltpu.make_async_copy(self.s3, self.r4.at[at.rep * 2 + at.core], self.d_r).start()
        for p in range(2):

            @pl.when(at.z != p)
            def _(p=p):
                drain(self.s3x.at[p], self.z_s.at[p])

        @pl.when(at.z < 2)
        def _():
            drain(self.r3.at[pl.ds(0, 8)], self.c_s)

        @pl.when(at.z >= 2)
        def _():
            drain(self.r3.at[pl.ds(0, 7)], self.c_s)

    def end(self):
        drain(self.r4, self.d_r)
        drain(self.r4.at[pl.ds(0, 7)], self.d_s)


def slot_positions(ct):
    me = lax.axis_index("dp")
    table = ct[:, 0, :]
    mine = jnp.where(iota((DP, DP), 1) == me, table, 0).astype(F32)
    counts = jnp.sum(mine, axis=1, keepdims=True)
    source = iota((DP, SLOTS), 0)
    slot_source = iota((DP, SLOTS), 1) // CAP
    start = jnp.sum(jnp.where(source < slot_source, counts, 0.0), axis=0, keepdims=True)
    count = jnp.sum(jnp.where(source == slot_source, counts, 0.0), axis=0, keepdims=True)
    within = lax.rem(iota((1, SLOTS), 1), CAP).astype(F32)
    return jnp.where(within < count, start + within, -1.0)


def compact(pos, rows_ref, out_ref):
    rows = rows_ref[...].reshape(SLOTS, N)
    for chunk in range(2):
        index = (iota((256, SLOTS), 0) + 256 * chunk).astype(F32)
        hot = onehot(index == pos)
        out_ref[256 * chunk : 256 * chunk + 256] = dot(hot, rows).astype(BF16)


def centred(values):
    center = values - jnp.mean(values, axis=-1, keepdims=True)
    spread = jnp.mean(center * center, axis=-1, keepdims=True)
    scale = lax.rsqrt(spread + EPSILON)
    return center * scale, scale


def norm_grad(grad, normed, scale):
    lead = jnp.mean(grad, axis=-1, keepdims=True)
    along = jnp.mean(grad * normed, axis=-1, keepdims=True)
    return scale * (grad - lead - normed * along)


def sigmoid(x):
    return 0.5 * jnp.tanh(0.5 * x) + 0.5


def allowed_mask(users, mask):
    row = users[...].astype(F32)
    column = column_of(row, N)
    for b in range(4):
        keys = slice(128 * b, 128 * b + 128)
        same = column == row[:, keys]
        causal = iota((N, 128), 1) + 128 * b <= iota((N, 128), 0)
        mask[:, keys] = onehot(same & causal)


def half_lanes(hh):
    return jnp.where(iota((1, 128), 1) // 64 == hh, 1.0, 0.0)


U, V, Q, K = (slice(128 * i, 128 * i + 128) for i in range(4))


def pair_forward(p, xh, wp, mask, act, slope, wt, gs, att):
    for half in range(2):
        cols = slice(256 * half, 256 * half + 256)
        pre = dot(xh[...], wp[p, :, cols])
        sig = sigmoid(pre)
        silu = pre * sig
        act[p, :, cols] = silu.astype(BF16)
        slope[p, :, cols] = (sig + silu * (1.0 - sig)).astype(BF16)
    v, q, k = act[p, :, V], act[p, :, Q], act[p, :, K]
    for t in range(2):
        rows = slice(256 * t, 256 * t + 256)
        nk = 256 * (t + 1)
        total = None
        for hh in range(2):
            lanes = half_lanes(hh)
            qm = q[rows] * lanes.astype(BF16)
            half = dot_nt(qm, k[:nk]) * 0.0625
            th = jnp.tanh(half)
            silu = half + half * th
            sig = 0.5 + 0.5 * th
            grad = (sig + silu * (1.0 - sig)) * 0.125
            ok = mask[rows, :nk]
            weights = silu.astype(BF16) * ok
            wt[2 * p + hh, rows, :nk] = weights
            gs[2 * p + hh, rows, :nk] = grad.astype(BF16) * ok
            out = dot(weights, v[:nk]) * lanes
            total = out if total is None else total + out
        att[rows, pl.ds(pl.multiple_of(128 * p, 128), 128)] = total


def pair_backward(p, act, slope, wt, gs, da, dpre):
    v, q, k = act[p, :, V], act[p, :, Q], act[p, :, K]
    d = da[:, pl.ds(pl.multiple_of(128 * p, 128), 128)]
    qt = jnp.transpose(q)
    dt = jnp.transpose(d)
    dvs, dks = [], []
    dq = [None, None]
    for hh in range(2):
        lanes = half_lanes(hh)
        half = slice(64 * hh, 64 * hh + 64)
        dv, dk = [], []
        for t in range(2):
            rows = slice(256 * t, 256 * t + 256)
            nk = 256 * (t + 1)
            dm = d[rows] * lanes.astype(BF16)
            dw = dot_nt(dm, v[:nk])
            ds = (dw * gs[2 * p + hh, rows, :nk].astype(F32)).astype(BF16)
            part = dot(ds, k[:nk]) * lanes
            dq[t] = part if dq[t] is None else dq[t] + part
            dk.append(dot(qt[half, rows], ds))
            dv.append(dot(dt[half, rows], wt[2 * p + hh, rows, :nk]))
        dks.append(jnp.concatenate([dk[0] + dk[1][:, :256], dk[1][:, 256:]], axis=1))
        dvs.append(jnp.concatenate([dv[0] + dv[1][:, :256], dv[1][:, 256:]], axis=1))
    for t in range(2):
        rows = slice(256 * t, 256 * t + 256)
        dpre[p, rows, Q] = dq[t].astype(BF16) * slope[p, rows, Q]
    dk = jnp.transpose(jnp.concatenate(dks, axis=0))
    dv = jnp.transpose(jnp.concatenate(dvs, axis=0))
    dpre[p, :, K] = dk.astype(BF16) * slope[p, :, K]
    dpre[p, :, V] = dv.astype(BF16) * slope[p, :, V]


def gate(att, scale, act, gated):
    for t in range(2):
        rows = slice(256 * t, 256 * t + 256)
        normed, by = centred(att[rows])
        u = jnp.concatenate([act[p, rows, U] for p in range(4)], axis=1).astype(F32)
        gated[rows] = (normed * u).astype(BF16)
        att[rows] = normed
        scale[rows] = jnp.broadcast_to(by, (256, 128))


def gate_grad(att, scale, act, slope, dy, wo, da, dpre):
    for t in range(2):
        rows = slice(256 * t, 256 * t + 256)
        normed = att[rows]
        u = jnp.concatenate([act[p, rows, U] for p in range(4)], axis=1).astype(F32)
        dg = dot_nt(dy[rows], wo[...]).astype(BF16).astype(F32)
        du = (dg * normed).astype(BF16)
        for p in range(4):
            dpre[p, rows, U] = du[:, 128 * p : 128 * p + 128] * slope[p, rows, U]
        da[rows] = norm_grad(dg * u, normed, scale[rows, 0:1]).astype(BF16)


def out_grad(dy, gated, g):
    term = dot(jnp.transpose(dy[...]), gated[...]).astype(BF16)
    term = term.reshape(CHIPS, 2, 16, N)
    for c in range(2):
        for y in range(4):
            g[c, 0, y] = term[:, c, :, 128 * y : 128 * y + 128].reshape(256, 128)


def pair_in_grad(p, xht, dpre, g):
    for half in range(2):
        term = dot(xht[...], dpre[p, :, 256 * half : 256 * half + 256]).astype(BF16)
        for x in range(2):
            for c in range(2):
                for y in range(4):
                    first = 256 * c + 64 * y
                    row = 64 * (2 * half + x)
                    g[c, 1 + p, y, row : row + 64, :] = term[
                        first : first + 64, 128 * x : 128 * x + 128
                    ]


def row_grad(x, dy, dpre, wp, dx):
    for t in range(2):
        rows = slice(256 * t, 256 * t + 256)
        dxh = dot_nt(dpre[0, rows], wp[0])
        for p in range(1, 4):
            dxh = dxh + dot_nt(dpre[p, rows], wp[p])
        dxh = dxh.astype(BF16).astype(F32)
        normed, scale = centred(x[rows].astype(F32))
        dx[rows] = (norm_grad(dxh, normed, scale) + dy[rows].astype(F32)).astype(BF16)


def spread(chunk, column, dx, out):
    part = column[pl.ds(pl.multiple_of(256 * chunk, 256), 256)]
    hot = jnp.concatenate(
        [onehot((iota((256, 128), 1) + 128 * b).astype(F32) == part) for b in range(4)], axis=1
    )
    out[pl.ds(8 * chunk, 8)] = dot(hot, dx[...]).astype(BF16).reshape(8, CAP, N)


def layer_kernel(
    ev_any, go_any, w_any, wo_any, place_any, cnt_any, users_any,
    ret, r4,
    place, cnt, users, ev, go, wp, wo, sx, sy, rx, ry, ct, dxp,
    x, dy, xh, xht, act, slope, mask, wt, gs, att, scale, da, dpre, gated, dx, column,
    g, r1, s1, r2, s2, r2x, s2x, r2y, s3x, r3, r3z, r3w, s3,
    load, xs, xr, ys, yr, cs, cr, bs, br, *sems,
):
    at = Place()
    barrier = pltpu.get_barrier_semaphore()
    small = [
        pltpu.make_async_copy(place_any, place, load.at[0]),
        pltpu.make_async_copy(ev_any, ev, load.at[1]),
        pltpu.make_async_copy(cnt_any, cnt, load.at[2]),
        pltpu.make_async_copy(users_any, users, load.at[3]),
        pltpu.make_async_copy(go_any, go, load.at[4]),
        pltpu.make_async_copy(wo_any, wo, load.at[5]),
    ]
    small[0].start()
    small[1].start()
    for dxo in (2, 1, 3, 0):
        each_peer(at, dxo, lambda peer: signal(barrier, peer, at.rep))
    for i in range(1, REP):
        for c in range(2):
            signal(barrier, at.chip * 2 + c, lax.rem(at.rep + i, REP))
    for copy in small[2:]:
        copy.start()
    for p in range(4):
        for i in range(4):
            pltpu.make_async_copy(
                w_any.at[:, pl.ds(512 * i + 128 * p, 128)],
                wp.at[p, :, pl.ds(128 * i, 128)],
                load.at[6],
            ).start()
    small[0].wait()
    small[1].wait()
    pack(place[...], ev[...], sx)
    to_x = Exchange(at, sx, rx, xs, xr)
    to_y = Exchange(at, sy, ry, ys, yr)
    counts = Exchange(at, cnt, ct, cs, cr, whole=True)
    back = Exchange(at, dxp, ret, bs, br)
    reduce = Reduce(
        at, (g, r1, s1, r2, s2, r2x, s2x, r2y, s3x, r3, r3z, r3w, s3, r4), sems
    )
    small[2].wait()
    pl.semaphore_wait(barrier, DP - 1 + 2 * (REP - 1))
    counts.start_all()
    to_x.start_all()
    small[4].wait()
    pack(place[...], go[...], sy)
    to_y.start_all()
    small[3].wait()
    allowed_mask(users, mask)
    counts.wait()
    pos = slot_positions(ct)
    column[...] = column_of(pos, SLOTS)
    small[5].wait()
    drain(wp, load.at[6])
    to_x.wait()
    compact(pos, rx, x)
    xh[...] = centred(x[...].astype(F32))[0].astype(BF16)
    xht[...] = jnp.transpose(xh[...])

    @pl.loop(0, 4)
    def _(p):
        pair_forward(p, xh, wp, mask, act, slope, wt, gs, att)

    gate(att, scale, act, gated)
    to_y.wait()
    compact(pos, ry, dy)
    gate_grad(att, scale, act, slope, dy, wo, da, dpre)
    out_grad(dy, gated, g)
    reduce.pair(0).start()
    for p in range(4):
        pair_backward(p, act, slope, wt, gs, da, dpre)
        pair_in_grad(p, xht, dpre, g)
        reduce.pair(1 + p).start()
        reduce.pair_done(p)
    row_grad(x, dy, dpre, wp, dx)
    steps = {
        2: lambda: reduce.pair_done(4),
        1: lambda: (reduce.y_done(0), reduce.out_start()),
        3: lambda: reduce.x_done(0),
        0: lambda: reduce.x_done(1),
    }
    for dxo in (2, 1, 3, 0):
        spread(lax.rem(at.x + dxo, 4), column, dx, dxp)
        back.start(dxo, (0, 2, 4, 6))
        steps[dxo]()
    reduce.y_done(3)
    reduce.columns_start(2)
    reduce.xy_done(0)
    reduce.xy_done(1)
    for dxo in (2, 1, 3, 0):
        back.start(dxo, (1, 5))
    reduce.y_done(4)
    reduce.columns_start(3)
    for dxo in (2, 1, 3, 0):
        back.start(dxo, (3, 7))
    reduce.finish()
    reduce.end()
    back.wait()


def finish_kernel(ret_any, r4_any, place, ge, gw, gout, ret, r4, sems):
    parts = [
        pltpu.make_async_copy(ret_any.at[pl.ds(8 * i, 8)], ret.at[pl.ds(8 * i, 8)], sems.at[i])
        for i in range(4)
    ]
    sums = pltpu.make_async_copy(r4_any, r4, sems.at[4])
    for copy in (*parts, sums):
        copy.start()
    core = lax.rem(lax.axis_index("dp"), 2)
    column = column_of(place[...].astype(F32), N)
    total = None
    for i in range(4):
        hot = jnp.concatenate(
            [onehot((iota((N, 128), 1) + 256 * i + 128 * b).astype(F32) == column) for b in range(2)],
            axis=1,
        )
        parts[i].wait()
        part = dot(hot, ret[8 * i : 8 * i + 8].reshape(256, N))
        total = part if total is None else total + part
    ge[...] = total.astype(BF16)
    sums.wait()
    for c in range(2):
        for half in range(2):
            block = jnp.concatenate([r4[4 * half + c, :64], r4[4 * half + 2 + c, :64]], axis=0)
            block = jnp.transpose(block.astype(F32))
            first = 256 * c + 128 * half
            gw[:, first : first + 128] = jnp.where(core == 1, block[64:], block[:64])
    for y in range(4):
        gout[:, 128 * y : 128 * y + 128] = r4[2 * y + core, 64:80].astype(F32)


DMA = pltpu.SemaphoreType.DMA
BLOCKS = pltpu.VMEM((DP, CAP, N), BF16)
SQUARE = pltpu.VMEM((N, N), BF16)
PAIRS = pltpu.VMEM((4, N, N), BF16)
TERMS = pltpu.VMEM((5, 4, 256, 128), BF16)
COLUMNS = pltpu.VMEM((2, 4, 64, 128), BF16)
SCRATCH = [
    pltpu.VMEM((1, N), I32), pltpu.VMEM((1, DP), I32), pltpu.VMEM((1, N), I32),
    SQUARE, SQUARE, PAIRS, SQUARE,
    BLOCKS, BLOCKS, BLOCKS, BLOCKS, pltpu.VMEM((DP, 1, DP), I32), BLOCKS,
    SQUARE, SQUARE, SQUARE, SQUARE, PAIRS, PAIRS, SQUARE,
    pltpu.VMEM((HEADS, N, N), BF16), pltpu.VMEM((HEADS, N, N), BF16),
    pltpu.VMEM((N, N), F32), pltpu.VMEM((N, 128), F32),
    SQUARE, PAIRS, SQUARE, SQUARE,
    pltpu.VMEM((SLOTS, 128), F32),
    pltpu.VMEM((2, 5, 4, 256, 128), BF16), TERMS, TERMS, TERMS,
    pltpu.VMEM((5, 256, 128), BF16),
    pltpu.VMEM((2, 4, 4, 64, 128), BF16), COLUMNS, COLUMNS,
    pltpu.VMEM((2, 64, 128), BF16),
    pltpu.VMEM((CHIPS, 64, 128), BF16), pltpu.VMEM((4, 64, 128), BF16),
    pltpu.VMEM((CHIPS, 16, 128), BF16), pltpu.VMEM((80, 128), BF16),
    DMA((7,)), DMA, DMA, DMA, DMA, DMA, DMA, DMA, DMA,
    DMA((5,)), DMA((5,)), DMA((5,)), DMA((5,)),
    DMA((2,)), DMA((2,)), DMA((2,)), DMA((2,)), DMA((2,)), DMA,
    DMA, DMA, DMA, DMA, DMA, DMA,
]
VM = pl.BlockSpec(memory_space=pltpu.VMEM)
ANY = pl.BlockSpec(memory_space=pl.ANY)


def on_device(events, grad_out, w_uvqk, w_out, send_place, send_counts, user_ids):
    ret, r4 = pl.pallas_call(
        layer_kernel,
        name="layer",
        out_shape=(
            jax.ShapeDtypeStruct((DP, CAP, N), BF16),
            jax.ShapeDtypeStruct((8, 80, 128), BF16),
        ),
        in_specs=[ANY] * 7,
        out_specs=(ANY,) * 2,
        scratch_shapes=SCRATCH,
        compiler_params=pltpu.CompilerParams(
            collective_id=0, has_side_effects=True, vmem_limit_bytes=VMEM_LIMIT
        ),
    )(events, grad_out, w_uvqk, w_out, send_place, send_counts, user_ids)
    ge, gw, gout = pl.pallas_call(
        finish_kernel,
        name="finish",
        out_shape=(
            jax.ShapeDtypeStruct((N, N), BF16),
            jax.ShapeDtypeStruct((64, N), F32),
            jax.ShapeDtypeStruct((16, N), F32),
        ),
        in_specs=[ANY, ANY, VM],
        out_specs=(VM,) * 3,
        scratch_shapes=[BLOCKS, pltpu.VMEM((8, 80, 128), BF16), DMA((5,))],
        compiler_params=pltpu.CompilerParams(vmem_limit_bytes=VMEM_LIMIT),
    )(ret, r4, send_place)
    return ge, gw.T, gout.T


def solution(mesh):
    rows = P(("dp", "rep"), None)
    return jax.shard_map(
        on_device,
        mesh=mesh,
        in_specs=(rows, rows, P(), P(), rows, rows, rows),
        out_specs=(rows, P(None, "dp"), P(None, "dp")),
        check_vma=False,
    )
```

```python
import jax
import jax.numpy as jnp
from jax import lax
from jax.experimental import pallas as pl
from jax.experimental.pallas import tpu as pltpu
from jax.sharding import PartitionSpec as P

HEADS = 8
EPSILON = 1e-05
F32 = jnp.float32
BF16 = jnp.bfloat16
I32 = jnp.int32
MESH = pl.DeviceIdType.MESH
N = 512
DP = 32
REP = 4
CAP = 32
SLOTS = 1024
CHIPS = 16
VMEM_LIMIT = 62 * 1024 * 1024


def dot(a, b):
    return jnp.dot(a, b, preferred_element_type=F32)


def dot_nt(a, b):
    return lax.dot_general(a, b, (((1,), (1,)), ((), ())), preferred_element_type=F32)


def iota(shape, dim):
    return lax.broadcasted_iota(I32, shape, dim)


def onehot(mask):
    return jnp.where(mask, 1.0, 0.0).astype(BF16)


def column_of(row, width):
    return jnp.transpose(jnp.broadcast_to(row, (128, width)))


def remote(src, dst, send, recv, dp, rep):
    return pltpu.make_async_remote_copy(
        src_ref=src,
        dst_ref=dst,
        send_sem=send,
        recv_sem=recv,
        device_id=(dp, rep),
        device_id_type=MESH,
    )


def signal(barrier, dp, rep):
    pl.semaphore_signal(barrier, 1, device_id=(dp, rep), device_id_type=MESH)


class Place:
    def __init__(self):
        self.me = lax.axis_index("dp")
        self.rep = lax.axis_index("rep")
        self.core = lax.rem(self.me, 2)
        self.chip = self.me // 2
        self.x = self.me // 8
        self.z = lax.rem(self.chip, 4)
        self.partner = self.chip * 2 + (1 - self.core)


def pack(chunk, place, rows, out):
    hot = onehot(iota((256, N), 0) + 256 * chunk == place[...])
    out[pl.ds(8 * chunk, 8)] = dot(hot, rows[...]).astype(BF16).reshape(8, CAP, N)


def each_peer(at, dx, body):
    column = lax.rem(at.x + dx, 4) * 8
    inner = lax.rem(at.me, 8)

    @pl.loop(0 if dx else 1, 8)
    def _(j):
        body(column + lax.rem(inner + j, 8))


def drain(ref, sem):
    pltpu.make_async_copy(ref, ref, sem).wait()


class Exchange:
    def __init__(self, at, src, dst, send, recv, whole=False):
        self.at, self.src, self.dst = at, src, dst
        self.send, self.recv, self.whole = send, recv, whole

    def block(self, peer):
        return self.src if self.whole else self.src.at[peer]

    def to(self, peer):
        at = self.at
        remote(self.block(peer), self.dst.at[at.me], self.send, self.recv, peer, at.rep).start()

    def own(self):
        me = self.at.me
        pltpu.make_async_copy(self.block(me), self.dst.at[me], self.recv).start()

    def start_column(self, dx):
        each_peer(self.at, dx, self.to)
        if dx == 0:
            self.own()

    def start(self, dx, steps):
        at = self.at
        column = lax.rem(at.x + dx, 4) * 8
        for j in steps:
            if dx == 0 and j == 0:
                self.own()
            else:
                self.to(column + lax.rem(lax.rem(at.me, 8) + j, 8))

    def wait(self):
        drain(self.dst, self.recv)
        drain(self.dst.at[pl.ds(0, DP - 1)], self.send)


class Reduce:
    def __init__(self, at, refs, sems):
        self.at = at
        (self.g, self.r1, self.s1, self.r2, self.s2, self.r2x, self.s2x, self.r2y, self.s3x,
         self.r5, self.r3z, self.rwx, self.s2w, self.rwy, self.s3, self.r4) = refs
        (self.a_s, self.a_r, self.b_s, self.b_r, self.x_s, self.x_r, self.y_s, self.y_r,
         self.z_s, self.z_r, self.e_s, self.e_r, self.w_s, self.w_r, self.v_s, self.v_r,
         self.d_s, self.d_r) = sems

    def pair(self, s):
        at = self.at
        return remote(
            self.g.at[1 - at.core, s], self.r1.at[s], self.a_s.at[s], self.a_r.at[s], at.partner, at.rep
        )

    def pair_done(self, s):
        at = self.at
        self.pair(s).wait()
        self.s1[s] = (self.g[at.core, s].astype(F32) + self.r1[s].astype(F32)).astype(BF16)
        for i in (2, 1, 3):
            if s in (2, 4):
                y = lax.rem(at.rep + i, REP)
                remote(
                    self.s1.at[s, y], self.r2.at[s, i], self.b_s.at[s], self.b_r.at[s], at.me, y
                ).start()
                continue
            t = 2 if s == 0 else s // 2
            other = lax.rem((at.z if s == 0 else at.x) + i, 4)
            to = at.x * 8 + other * 2 + at.core if s == 0 else other * 8 + lax.rem(at.me, 8)
            remote(
                self.s1.at[s, :, pl.ds(pl.multiple_of(64 * other, 64), 64)], self.r2x.at[t, i],
                self.x_s.at[t], self.x_r.at[t], to, at.rep,
            ).start()

    def y_done(self, s):
        at = self.at
        drain(self.r2.at[s, pl.ds(1, 3)], self.b_r.at[s])
        drain(self.r2.at[s, pl.ds(1, 3)], self.b_s.at[s])
        total = self.s1[s, self.at.rep].astype(F32)
        for i in (1, 2, 3):
            total = total + self.r2[s, i].astype(F32)
        self.s2[s] = total.astype(BF16)
        u = s // 2 - 1
        for i in (2, 1, 3):
            x = lax.rem(at.x + i, 4)
            remote(
                self.s2.at[s, pl.ds(pl.multiple_of(64 * x, 64), 64)], self.r5.at[u, i],
                self.e_s.at[u], self.e_r.at[u], x * 8 + lax.rem(at.me, 8), at.rep,
            ).start()

    def yx_done(self, s):
        u = s // 2 - 1
        drain(self.r5.at[u, pl.ds(1, 3)], self.e_r.at[u])
        drain(self.r5.at[u, pl.ds(1, 3)], self.e_s.at[u])
        total = self.s2[s, pl.ds(pl.multiple_of(64 * self.at.x, 64), 64)].astype(F32)
        for i in (1, 2, 3):
            total = total + self.r5[u, i].astype(F32)
        self.to_z(s - 1, total)

    def to_z(self, p, total):
        at = self.at
        self.s3x[p] = total.astype(BF16)

        @pl.when(at.z != p)
        def _():
            to = at.x * 4 + p
            remote(
                self.s3x.at[p], self.r3z.at[at.z], self.z_s.at[p], self.z_r, to * 2 + at.core, at.rep
            ).start()

    def first_sum(self, t):
        at = self.at
        s, own = (0, at.z) if t == 2 else (1 + 2 * t, at.x)
        drain(self.r2x.at[t, pl.ds(1, 3)], self.x_r.at[t])
        drain(self.r2x.at[t, pl.ds(1, 3)], self.x_s.at[t])
        total = self.s1[s, :, pl.ds(pl.multiple_of(64 * own, 64), 64)].astype(F32)
        for i in (1, 2, 3):
            total = total + self.r2x[t, i].astype(F32)
        self.s2x[t] = total.astype(BF16)

    def x_done(self, t):
        at = self.at
        self.first_sum(t)
        for i in (2, 1, 3):
            y = lax.rem(at.rep + i, REP)
            remote(
                self.s2x.at[t, y], self.r2y.at[t, i], self.y_s.at[t], self.y_r.at[t], at.me, y
            ).start()

    def xy_done(self, t):
        drain(self.r2y.at[t, pl.ds(1, 3)], self.y_r.at[t])
        drain(self.r2y.at[t, pl.ds(1, 3)], self.y_s.at[t])
        total = self.s2x[t, self.at.rep].astype(F32)
        for i in (1, 2, 3):
            total = total + self.r2y[t, i].astype(F32)
        self.to_z(2 * t, total)

    def out_x_start(self):
        at = self.at
        self.first_sum(2)
        for i in (2, 1, 3):
            x = lax.rem(at.x + i, 4)
            remote(
                self.s2x.at[2, :, pl.ds(pl.multiple_of(16 * x, 16), 16)], self.rwx.at[i],
                self.w_s, self.w_r, x * 8 + lax.rem(at.me, 8), at.rep,
            ).start()

    def out_y_start(self):
        at = self.at
        drain(self.rwx.at[pl.ds(1, 3)], self.w_r)
        drain(self.rwx.at[pl.ds(1, 3)], self.w_s)
        total = self.s2x[2, :, pl.ds(pl.multiple_of(16 * at.x, 16), 16)].astype(F32)
        for i in (1, 2, 3):
            total = total + self.rwx[i].astype(F32)
        self.s2w[...] = total.astype(BF16)
        for i in (2, 1, 3):
            y = lax.rem(at.rep + i, REP)
            remote(self.s2w.at[y], self.rwy.at[i], self.v_s, self.v_r, at.me, y).start()

    def total(self, ref, count, rows):
        total = ref[0].astype(F32)
        for i in range(1, count):
            total = total + ref[i].astype(F32)
        self.s3[rows] = total.astype(BF16)

    def finish(self):
        at = self.at
        drain(self.rwy.at[pl.ds(1, 3)], self.v_r)
        drain(self.rwy.at[pl.ds(1, 3)], self.v_s)
        self.rwy[0] = self.s2w[at.rep]
        self.total(self.rwy, 4, slice(64, 80))

        drain(self.r3z.at[pl.ds(0, 3)], self.z_r)
        self.r3z[at.z] = self.s3x[at.z]
        self.total(self.r3z, 4, slice(0, 64))
        mine = self.r4.at[at.rep * 2 + at.core]
        for i in (2, 1, 3, 0):
            for core in (1 - at.core, at.core):
                if i or core is not at.core:
                    y = lax.rem(at.rep + i, REP)
                    remote(self.s3, mine, self.d_s, self.d_r, at.chip * 2 + core, y).start()
        pltpu.make_async_copy(self.s3, mine, self.d_r).start()
        for p in range(4):

            @pl.when(at.z != p)
            def _(p=p):
                drain(self.s3x.at[p], self.z_s.at[p])

    def end(self):
        drain(self.r4, self.d_r)
        drain(self.r4.at[pl.ds(0, 7)], self.d_s)


def slot_positions(ct):
    me = lax.axis_index("dp")
    table = ct[:, 0, :]
    mine = jnp.where(iota((DP, DP), 1) == me, table, 0).astype(F32)
    counts = jnp.sum(mine, axis=1, keepdims=True)
    source = iota((DP, SLOTS), 0)
    slot_source = iota((DP, SLOTS), 1) // CAP
    start = jnp.sum(jnp.where(source < slot_source, counts, 0.0), axis=0, keepdims=True)
    count = jnp.sum(jnp.where(source == slot_source, counts, 0.0), axis=0, keepdims=True)
    within = lax.rem(iota((1, SLOTS), 1), CAP).astype(F32)
    return jnp.where(within < count, start + within, -1.0)


def compact(pos, rows_ref, out_ref):
    rows = rows_ref[...].reshape(SLOTS, N)
    for chunk in range(2):
        slots = slice(256 * chunk, 256 * chunk + 768)
        index = (iota((256, 768), 0) + 256 * chunk).astype(F32)
        hot = onehot(index == pos[:, slots])
        out_ref[256 * chunk : 256 * chunk + 256] = dot(hot, rows[slots]).astype(BF16)


def centred(values):
    center = values - jnp.mean(values, axis=-1, keepdims=True)
    spread = jnp.mean(center * center, axis=-1, keepdims=True)
    scale = lax.rsqrt(spread + EPSILON)
    return center * scale, scale


def norm_grad(grad, normed, scale):
    lead = jnp.mean(grad, axis=-1, keepdims=True)
    along = jnp.mean(grad * normed, axis=-1, keepdims=True)
    return scale * (grad - lead - normed * along)


def sigmoid(x):
    return 0.5 * jnp.tanh(0.5 * x) + 0.5


def allowed_mask(users, mask):
    row = users[...].astype(F32)
    column = column_of(row, N)
    for b in range(4):
        keys = slice(128 * b, 128 * b + 128)
        same = column == row[:, keys]
        causal = iota((N, 128), 1) + 128 * b <= iota((N, 128), 0)
        mask[:, keys] = onehot(same & causal)


def half_lanes(hh):
    return jnp.where(iota((1, 128), 1) // 64 == hh, 1.0, 0.0)


U, V, Q, K = (slice(128 * i, 128 * i + 128) for i in range(4))


def pair_forward(p, xh, wp, mask, act, slope, wt, gs, att):
    for half in range(2):
        cols = slice(256 * half, 256 * half + 256)
        pre = dot(xh[...], wp[p, :, cols])
        sig = sigmoid(pre)
        silu = pre * sig
        act[p, :, cols] = silu.astype(BF16)
        slope[p, :, cols] = (sig + silu * (1.0 - sig)).astype(BF16)
    v, q, k = act[p, :, V], act[p, :, Q], act[p, :, K]
    for t in range(2):
        rows = slice(256 * t, 256 * t + 256)
        nk = 256 * (t + 1)
        total = None
        for hh in range(2):
            lanes = half_lanes(hh)
            qm = q[rows] * lanes.astype(BF16)
            half = dot_nt(qm, k[:nk]) * 0.0625
            th = jnp.tanh(half)
            silu = half + half * th
            sig = 0.5 + 0.5 * th
            grad = (sig + silu * (1.0 - sig)) * 0.125
            ok = mask[rows, :nk]
            weights = silu.astype(BF16) * ok
            wt[2 * p + hh, rows, :nk] = weights
            gs[2 * p + hh, rows, :nk] = grad.astype(BF16) * ok
            out = dot(weights, v[:nk]) * lanes
            total = out if total is None else total + out
        att[rows, pl.ds(pl.multiple_of(128 * p, 128), 128)] = total


def pair_backward(p, act, slope, wt, gs, da, dpre):
    v, q, k = act[p, :, V], act[p, :, Q], act[p, :, K]
    d = da[:, pl.ds(pl.multiple_of(128 * p, 128), 128)]
    qt = jnp.transpose(q)
    dt = jnp.transpose(d)
    dvs, dks = [], []
    dq = [None, None]
    for hh in range(2):
        lanes = half_lanes(hh)
        half = slice(64 * hh, 64 * hh + 64)
        dv, dk = [], []
        for t in range(2):
            rows = slice(256 * t, 256 * t + 256)
            nk = 256 * (t + 1)
            dm = d[rows] * lanes.astype(BF16)
            dw = dot_nt(dm, v[:nk])
            ds = (dw * gs[2 * p + hh, rows, :nk].astype(F32)).astype(BF16)
            part = dot(ds, k[:nk]) * lanes
            dq[t] = part if dq[t] is None else dq[t] + part
            dk.append(dot(qt[half, rows], ds))
            dv.append(dot(dt[half, rows], wt[2 * p + hh, rows, :nk]))
        dks.append(jnp.concatenate([dk[0] + dk[1][:, :256], dk[1][:, 256:]], axis=1))
        dvs.append(jnp.concatenate([dv[0] + dv[1][:, :256], dv[1][:, 256:]], axis=1))
    for t in range(2):
        rows = slice(256 * t, 256 * t + 256)
        dpre[p, rows, Q] = dq[t].astype(BF16) * slope[p, rows, Q]
    dk = jnp.transpose(jnp.concatenate(dks, axis=0))
    dv = jnp.transpose(jnp.concatenate(dvs, axis=0))
    dpre[p, :, K] = dk.astype(BF16) * slope[p, :, K]
    dpre[p, :, V] = dv.astype(BF16) * slope[p, :, V]


def gate(att, scale, act, gated):
    for t in range(2):
        rows = slice(256 * t, 256 * t + 256)
        normed, by = centred(att[rows])
        u = jnp.concatenate([act[p, rows, U] for p in range(4)], axis=1).astype(F32)
        gated[rows] = (normed * u).astype(BF16)
        att[rows] = normed
        scale[rows] = jnp.broadcast_to(by, (256, 128))


def gate_grad(att, scale, act, slope, dy, wo, da, dpre):
    for t in range(2):
        rows = slice(256 * t, 256 * t + 256)
        normed = att[rows]
        u = jnp.concatenate([act[p, rows, U] for p in range(4)], axis=1).astype(F32)
        dg = dot_nt(dy[rows], wo[...]).astype(BF16).astype(F32)
        du = (dg * normed).astype(BF16)
        for p in range(4):
            dpre[p, rows, U] = du[:, 128 * p : 128 * p + 128] * slope[p, rows, U]
        da[rows] = norm_grad(dg * u, normed, scale[rows, 0:1]).astype(BF16)


def out_grad(dy, gated, g):
    term = dot(jnp.transpose(dy[...]), gated[...]).astype(BF16)
    for chip in range(CHIPS):
        first = 64 * (chip % 4) + 16 * (chip // 4)
        for c in range(2):
            row = 32 * chip + 16 * c
            for y in range(4):
                g[c, 0, y, first : first + 16, :] = term[row : row + 16, 128 * y : 128 * y + 128]


def pair_in_grad(p, xht, dpre, g):
    for half in range(2):
        term = dot(xht[...], dpre[p, :, 256 * half : 256 * half + 256]).astype(BF16)
        for x in range(2):
            for c in range(2):
                for y in range(4):
                    first = 256 * c + 64 * y
                    row = 64 * (2 * half + x)
                    g[c, 1 + p, y, row : row + 64, :] = term[
                        first : first + 64, 128 * x : 128 * x + 128
                    ]


def row_grad(xn, xscale, dy, dpre, wp, dx):
    for t in range(2):
        rows = slice(256 * t, 256 * t + 256)
        dxh = dot_nt(dpre[0, rows], wp[0])
        for p in range(1, 4):
            dxh = dxh + dot_nt(dpre[p, rows], wp[p])
        dxh = dxh.astype(BF16).astype(F32)
        grad = norm_grad(dxh, xn[rows], xscale[rows, 0:1])
        dx[rows] = (grad + dy[rows].astype(F32)).astype(BF16)


def spread(chunk, column, dx, out):
    part = column[pl.ds(pl.multiple_of(256 * chunk, 256), 256)]
    hot = jnp.concatenate(
        [onehot((iota((256, 128), 1) + 128 * b).astype(F32) == part) for b in range(4)], axis=1
    )
    out[pl.ds(8 * chunk, 8)] = dot(hot, dx[...]).astype(BF16).reshape(8, CAP, N)


def layer_kernel(
    ev_any, go_any, w_any, wo_any, place_any, cnt_any, users_any,
    ret, r4,
    place, cnt, users, ev, go, wp, wo, sx, sy, rx, ry, ct, dxp,
    x, xn, xscale, dy, xh, xht, act, slope, mask, wt, gs, att, scale, da, dpre, gated, dx, column,
    g, r1, s1, r2, s2, r2x, s2x, r2y, s3x, r5, r3z, rwx, s2w, rwy, s3,
    load, xs, xr, ys, yr, cs, cr, bs, br, *sems,
):
    at = Place()
    barrier = pltpu.get_barrier_semaphore()
    small = [
        pltpu.make_async_copy(place_any, place, load.at[0]),
        pltpu.make_async_copy(ev_any, ev, load.at[1]),
        pltpu.make_async_copy(cnt_any, cnt, load.at[2]),
        pltpu.make_async_copy(users_any, users, load.at[3]),
        pltpu.make_async_copy(go_any, go, load.at[4]),
        pltpu.make_async_copy(wo_any, wo, load.at[5]),
    ]
    small[0].start()
    small[1].start()
    for dxo in (2, 1, 3, 0):
        each_peer(at, dxo, lambda peer: signal(barrier, peer, at.rep))
    for i in range(1, REP):
        for c in range(2):
            signal(barrier, at.chip * 2 + c, lax.rem(at.rep + i, REP))
    for copy in small[2:]:
        copy.start()
    for p in range(4):
        for i in range(4):
            pltpu.make_async_copy(
                w_any.at[:, pl.ds(512 * i + 128 * p, 128)],
                wp.at[p, :, pl.ds(128 * i, 128)],
                load.at[6],
            ).start()
    small[0].wait()
    small[1].wait()
    to_x = Exchange(at, sx, rx, xs, xr)
    to_y = Exchange(at, sy, ry, ys, yr)
    counts = Exchange(at, cnt, ct, cs, cr, whole=True)
    back = Exchange(at, dxp, ret, bs, br)
    reduce = Reduce(
        at, (g, r1, s1, r2, s2, r2x, s2x, r2y, s3x, r5, r3z, rwx, s2w, rwy, s3, r4), sems
    )
    columns = (2, 1, 3, 0)
    pack(lax.rem(at.x + 2, 4), place, ev, sx)
    small[2].wait()
    pl.semaphore_wait(barrier, DP - 1 + 2 * (REP - 1))
    for dxo in columns:
        counts.start_column(dxo)
    to_x.start_column(2)
    for dxo in (1, 3, 0):
        pack(lax.rem(at.x + dxo, 4), place, ev, sx)
        to_x.start_column(dxo)
    small[4].wait()
    for dxo in columns:
        pack(lax.rem(at.x + dxo, 4), place, go, sy)
    small[3].wait()
    allowed_mask(users, mask)
    counts.wait()
    for dxo in columns:
        to_y.start_column(dxo)
    pos = slot_positions(ct)
    column[...] = column_of(pos, SLOTS)
    small[5].wait()
    drain(wp, load.at[6])
    to_x.wait()
    compact(pos, rx, x)
    normed, by = centred(x[...].astype(F32))
    xn[...] = normed
    xscale[...] = jnp.broadcast_to(by, (N, 128))
    xh[...] = normed.astype(BF16)
    xht[...] = jnp.transpose(xh[...])

    @pl.loop(0, 4)
    def _(p):
        pair_forward(p, xh, wp, mask, act, slope, wt, gs, att)

    gate(att, scale, act, gated)
    to_y.wait()
    compact(pos, ry, dy)
    gate_grad(att, scale, act, slope, dy, wo, da, dpre)
    out_grad(dy, gated, g)
    reduce.pair(0).start()
    for p in range(4):
        pair_backward(p, act, slope, wt, gs, da, dpre)
        pair_in_grad(p, xht, dpre, g)
        reduce.pair(1 + p).start()
        reduce.pair_done(p)
    row_grad(xn, xscale, dy, dpre, wp, dx)
    for dxo in columns:
        spread(lax.rem(at.x + dxo, 4), column, dx, dxp)
        back.start(dxo, (0, 2, 4))
        if dxo == 2:
            reduce.pair_done(4)
    reduce.x_done(0)
    reduce.out_x_start()
    reduce.y_done(2)
    reduce.xy_done(0)
    for dxo in columns:
        back.start(dxo, (6,))
    reduce.x_done(1)
    reduce.out_y_start()
    reduce.y_done(4)
    for dxo in columns:
        back.start(dxo, (1, 5))
    reduce.yx_done(2)
    reduce.xy_done(1)
    for dxo in columns:
        back.start(dxo, (3,))
    reduce.yx_done(4)
    for dxo in columns:
        back.start(dxo, (7,))
    reduce.finish()
    reduce.end()
    back.wait()


def finish_kernel(ret, r4, place, ge_any, gw_any, gout_any, ge, gw, gout, sems):
    core = lax.rem(lax.axis_index("dp"), 2)
    column = column_of(place[...].astype(F32), N)
    stores = []
    for t in range(2):
        rows = slice(256 * t, 256 * t + 256)
        hot = jnp.concatenate(
            [onehot((iota((256, 128), 1) + 128 * b).astype(F32) == column[rows]) for b in range(8)],
            axis=1,
        )
        ge[rows] = dot(hot, ret[...].reshape(SLOTS, N)).astype(BF16)
        part = pl.ds(256 * t, 256)
        stores.append(pltpu.make_async_copy(ge.at[part], ge_any.at[part], sems.at[t]))
        stores[-1].start()
    for c in range(2):
        for half in range(2):
            block = jnp.concatenate([r4[4 * half + c, :64], r4[4 * half + 2 + c, :64]], axis=0)
            block = jnp.transpose(block.astype(F32))
            first = 256 * c + 128 * half
            gw[:, first : first + 128] = jnp.where(core == 1, block[64:], block[:64])
    for y in range(4):
        gout[:, 128 * y : 128 * y + 128] = r4[2 * y + core, 64:80].astype(F32)
    stores.append(pltpu.make_async_copy(gw, gw_any, sems.at[2]))
    stores.append(pltpu.make_async_copy(gout, gout_any, sems.at[3]))
    stores[2].start()
    stores[3].start()
    for copy in stores:
        copy.wait()


DMA = pltpu.SemaphoreType.DMA
BLOCKS = pltpu.VMEM((DP, CAP, N), BF16)
SQUARE = pltpu.VMEM((N, N), BF16)
PAIRS = pltpu.VMEM((4, N, N), BF16)
TERMS = pltpu.VMEM((5, 4, 256, 128), BF16)
COLUMNS = pltpu.VMEM((2, 4, 64, 128), BF16)
SCRATCH = [
    pltpu.VMEM((1, N), I32), pltpu.VMEM((1, DP), I32), pltpu.VMEM((1, N), I32),
    SQUARE, SQUARE, PAIRS, SQUARE,
    BLOCKS, BLOCKS, BLOCKS, BLOCKS, pltpu.VMEM((DP, 1, DP), I32), BLOCKS,
    SQUARE, pltpu.VMEM((N, N), F32), pltpu.VMEM((N, 128), F32),
    SQUARE, SQUARE, SQUARE, PAIRS, PAIRS, SQUARE,
    pltpu.VMEM((HEADS, N, N), BF16), pltpu.VMEM((HEADS, N, N), BF16),
    pltpu.VMEM((N, N), F32), pltpu.VMEM((N, 128), F32),
    SQUARE, PAIRS, SQUARE, SQUARE,
    pltpu.VMEM((SLOTS, 128), F32),
    pltpu.VMEM((2, 5, 4, 256, 128), BF16), TERMS, TERMS, TERMS,
    pltpu.VMEM((5, 256, 128), BF16),
    pltpu.VMEM((3, 4, 4, 64, 128), BF16), pltpu.VMEM((3, 4, 64, 128), BF16), COLUMNS,
    pltpu.VMEM((4, 64, 128), BF16),
    pltpu.VMEM((2, 4, 64, 128), BF16), pltpu.VMEM((4, 64, 128), BF16),
    pltpu.VMEM((4, 4, 16, 128), BF16), pltpu.VMEM((4, 16, 128), BF16),
    pltpu.VMEM((4, 16, 128), BF16), pltpu.VMEM((80, 128), BF16),
    DMA((7,)), DMA, DMA, DMA, DMA, DMA, DMA, DMA, DMA,
    DMA((5,)), DMA((5,)), DMA((5,)), DMA((5,)),
    DMA((3,)), DMA((3,)), DMA((2,)), DMA((2,)), DMA((4,)), DMA,
    DMA((2,)), DMA((2,)), DMA, DMA, DMA, DMA, DMA, DMA,
]
VM = pl.BlockSpec(memory_space=pltpu.VMEM)
ANY = pl.BlockSpec(memory_space=pl.ANY)


def on_device(events, grad_out, w_uvqk, w_out, send_place, send_counts, user_ids):
    ret, r4 = pl.pallas_call(
        layer_kernel,
        name="layer",
        out_shape=(pltpu.VMEM((DP, CAP, N), BF16), pltpu.VMEM((8, 80, 128), BF16)),
        in_specs=[ANY] * 7,
        out_specs=(VM,) * 2,
        scratch_shapes=SCRATCH,
        compiler_params=pltpu.CompilerParams(
            collective_id=0, has_side_effects=True, vmem_limit_bytes=VMEM_LIMIT
        ),
    )(events, grad_out, w_uvqk, w_out, send_place, send_counts, user_ids)
    ge, gw, gout = pl.pallas_call(
        finish_kernel,
        name="finish",
        out_shape=(
            jax.ShapeDtypeStruct((N, N), BF16),
            jax.ShapeDtypeStruct((64, N), F32),
            jax.ShapeDtypeStruct((16, N), F32),
        ),
        in_specs=[VM] * 3,
        out_specs=(ANY,) * 3,
        scratch_shapes=[
            SQUARE, pltpu.VMEM((64, N), F32), pltpu.VMEM((16, N), F32), DMA((4,)),
        ],
        compiler_params=pltpu.CompilerParams(vmem_limit_bytes=16 * 1024 * 1024),
    )(ret, r4, send_place)
    return ge, gw.T, gout.T


def solution(mesh):
    rows = P(("dp", "rep"), None)
    return jax.shard_map(
        on_device,
        mesh=mesh,
        in_specs=(rows, rows, P(), P(), rows, rows, rows),
        out_specs=(rows, P(None, "dp"), P(None, "dp")),
        check_vma=False,
    )
```

```python
import jax
import jax.numpy as jnp
from jax import lax
from jax.experimental import pallas as pl
from jax.experimental.pallas import tpu as pltpu
from jax.sharding import PartitionSpec as P

HEADS = 8
EPSILON = 1e-05
F32 = jnp.float32
BF16 = jnp.bfloat16
I32 = jnp.int32
MESH = pl.DeviceIdType.MESH
N = 512
DP = 32
REP = 4
CAP = 32
SLOTS = 1024
CHIPS = 16
VMEM_LIMIT = 62 * 1024 * 1024


def dot(a, b):
    return jnp.dot(a, b, preferred_element_type=F32)


def dot_nt(a, b):
    return lax.dot_general(a, b, (((1,), (1,)), ((), ())), preferred_element_type=F32)


def iota(shape, dim):
    return lax.broadcasted_iota(I32, shape, dim)


def onehot(mask):
    return jnp.where(mask, 1.0, 0.0).astype(BF16)


def column_of(row, width):
    return jnp.transpose(jnp.broadcast_to(row, (128, width)))


def remote(src, dst, send, recv, dp, rep):
    return pltpu.make_async_remote_copy(
        src_ref=src,
        dst_ref=dst,
        send_sem=send,
        recv_sem=recv,
        device_id=(dp, rep),
        device_id_type=MESH,
    )


def signal(barrier, dp, rep):
    pl.semaphore_signal(barrier, 1, device_id=(dp, rep), device_id_type=MESH)


class Place:
    def __init__(self):
        self.me = lax.axis_index("dp")
        self.rep = lax.axis_index("rep")
        self.core = lax.rem(self.me, 2)
        self.chip = self.me // 2
        self.x = self.me // 8
        self.z = lax.rem(self.chip, 4)
        self.partner = self.chip * 2 + (1 - self.core)


def pack(chunk, place, rows, out):
    hot = onehot(iota((256, N), 0) + 256 * chunk == place[...])
    out[pl.ds(8 * chunk, 8)] = dot(hot, rows[...]).astype(BF16).reshape(8, CAP, N)


def each_peer(at, dx, body):
    column = lax.rem(at.x + dx, 4) * 8
    inner = lax.rem(at.me, 8)

    @pl.loop(0 if dx else 1, 8)
    def _(j):
        body(column + lax.rem(inner + j, 8))


def drain(ref, sem):
    pltpu.make_async_copy(ref, ref, sem).wait()


class Exchange:
    def __init__(self, at, src, dst, send, recv, whole=False):
        self.at, self.src, self.dst = at, src, dst
        self.send, self.recv, self.whole = send, recv, whole

    def block(self, peer):
        return self.src if self.whole else self.src.at[peer]

    def to(self, peer):
        at = self.at
        remote(self.block(peer), self.dst.at[at.me], self.send, self.recv, peer, at.rep).start()

    def own(self):
        me = self.at.me
        pltpu.make_async_copy(self.block(me), self.dst.at[me], self.recv).start()

    def start_column(self, dx):
        each_peer(self.at, dx, self.to)
        if dx == 0:
            self.own()

    def start(self, dx, steps):
        at = self.at
        column = lax.rem(at.x + dx, 4) * 8
        for j in steps:
            if dx == 0 and j == 0:
                self.own()
            else:
                self.to(column + lax.rem(lax.rem(at.me, 8) + j, 8))

    def wait(self):
        drain(self.dst, self.recv)
        drain(self.dst.at[pl.ds(0, DP - 1)], self.send)


class Reduce:
    def __init__(self, at, refs, sems):
        self.at = at
        (self.g, self.r1, self.s1, self.r2, self.s2, self.r2x, self.s2x, self.r2y, self.s3x,
         self.r5, self.r3z, self.rwx, self.s2w, self.rwy, self.s3, self.r4) = refs
        (self.a_s, self.a_r, self.b_s, self.b_r, self.x_s, self.x_r, self.y_s, self.y_r,
         self.z_s, self.z_r, self.e_s, self.e_r, self.w_s, self.w_r, self.v_s, self.v_r,
         self.d_s, self.d_r) = sems

    def pair(self, s):
        at = self.at
        return remote(
            self.g.at[1 - at.core, s], self.r1.at[s], self.a_s.at[s], self.a_r.at[s], at.partner, at.rep
        )

    def pair_done(self, s):
        at = self.at
        self.pair(s).wait()
        self.s1[s] = (self.g[at.core, s].astype(F32) + self.r1[s].astype(F32)).astype(BF16)
        for i in (2, 1, 3):
            if s in (2, 4):
                y = lax.rem(at.rep + i, REP)
                remote(
                    self.s1.at[s, y], self.r2.at[s, i], self.b_s.at[s], self.b_r.at[s], at.me, y
                ).start()
                continue
            t = 2 if s == 0 else s // 2
            other = lax.rem((at.z if s == 0 else at.x) + i, 4)
            to = at.x * 8 + other * 2 + at.core if s == 0 else other * 8 + lax.rem(at.me, 8)
            remote(
                self.s1.at[s, :, pl.ds(pl.multiple_of(64 * other, 64), 64)], self.r2x.at[t, i],
                self.x_s.at[t], self.x_r.at[t], to, at.rep,
            ).start()

    def y_done(self, s):
        at = self.at
        drain(self.r2.at[s, pl.ds(1, 3)], self.b_r.at[s])
        drain(self.r2.at[s, pl.ds(1, 3)], self.b_s.at[s])
        total = self.s1[s, self.at.rep].astype(F32)
        for i in (1, 2, 3):
            total = total + self.r2[s, i].astype(F32)
        self.s2[s] = total.astype(BF16)
        u = s // 2 - 1
        for i in (2, 1, 3):
            x = lax.rem(at.x + i, 4)
            remote(
                self.s2.at[s, pl.ds(pl.multiple_of(64 * x, 64), 64)], self.r5.at[u, i],
                self.e_s.at[u], self.e_r.at[u], x * 8 + lax.rem(at.me, 8), at.rep,
            ).start()

    def yx_done(self, s):
        u = s // 2 - 1
        drain(self.r5.at[u, pl.ds(1, 3)], self.e_r.at[u])
        drain(self.r5.at[u, pl.ds(1, 3)], self.e_s.at[u])
        total = self.s2[s, pl.ds(pl.multiple_of(64 * self.at.x, 64), 64)].astype(F32)
        for i in (1, 2, 3):
            total = total + self.r5[u, i].astype(F32)
        self.to_z(s - 1, total)

    def to_z(self, p, total):
        at = self.at
        self.s3x[p] = total.astype(BF16)

        @pl.when(at.z != p)
        def _():
            to = at.x * 4 + p
            remote(
                self.s3x.at[p], self.r3z.at[at.z], self.z_s.at[p], self.z_r, to * 2 + at.core, at.rep
            ).start()

    def first_sum(self, t):
        at = self.at
        s, own = (0, at.z) if t == 2 else (1 + 2 * t, at.x)
        drain(self.r2x.at[t, pl.ds(1, 3)], self.x_r.at[t])
        drain(self.r2x.at[t, pl.ds(1, 3)], self.x_s.at[t])
        total = self.s1[s, :, pl.ds(pl.multiple_of(64 * own, 64), 64)].astype(F32)
        for i in (1, 2, 3):
            total = total + self.r2x[t, i].astype(F32)
        self.s2x[t] = total.astype(BF16)

    def x_done(self, t):
        at = self.at
        self.first_sum(t)
        for i in (2, 1, 3):
            y = lax.rem(at.rep + i, REP)
            remote(
                self.s2x.at[t, y], self.r2y.at[t, i], self.y_s.at[t], self.y_r.at[t], at.me, y
            ).start()

    def xy_done(self, t):
        drain(self.r2y.at[t, pl.ds(1, 3)], self.y_r.at[t])
        drain(self.r2y.at[t, pl.ds(1, 3)], self.y_s.at[t])
        total = self.s2x[t, self.at.rep].astype(F32)
        for i in (1, 2, 3):
            total = total + self.r2y[t, i].astype(F32)
        self.to_z(2 * t, total)

    def out_x_start(self):
        at = self.at
        self.first_sum(2)
        for i in (2, 1, 3):
            x = lax.rem(at.x + i, 4)
            remote(
                self.s2x.at[2, :, pl.ds(pl.multiple_of(16 * x, 16), 16)], self.rwx.at[i],
                self.w_s, self.w_r, x * 8 + lax.rem(at.me, 8), at.rep,
            ).start()

    def out_y_start(self):
        at = self.at
        drain(self.rwx.at[pl.ds(1, 3)], self.w_r)
        drain(self.rwx.at[pl.ds(1, 3)], self.w_s)
        total = self.s2x[2, :, pl.ds(pl.multiple_of(16 * at.x, 16), 16)].astype(F32)
        for i in (1, 2, 3):
            total = total + self.rwx[i].astype(F32)
        self.s2w[...] = total.astype(BF16)
        for i in (2, 1, 3):
            y = lax.rem(at.rep + i, REP)
            remote(self.s2w.at[y], self.rwy.at[i], self.v_s, self.v_r, at.me, y).start()

    def total(self, ref, count, rows):
        total = ref[0].astype(F32)
        for i in range(1, count):
            total = total + ref[i].astype(F32)
        self.s3[rows] = total.astype(BF16)

    def finish(self):
        at = self.at
        drain(self.rwy.at[pl.ds(1, 3)], self.v_r)
        drain(self.rwy.at[pl.ds(1, 3)], self.v_s)
        self.rwy[0] = self.s2w[at.rep]
        self.total(self.rwy, 4, slice(64, 80))

        drain(self.r3z.at[pl.ds(0, 3)], self.z_r)
        self.r3z[at.z] = self.s3x[at.z]
        self.total(self.r3z, 4, slice(0, 64))
        mine = self.r4.at[at.rep * 2 + at.core]
        for i in (2, 1, 3, 0):
            for core in (1 - at.core, at.core):
                if i or core is not at.core:
                    y = lax.rem(at.rep + i, REP)
                    remote(self.s3, mine, self.d_s, self.d_r, at.chip * 2 + core, y).start()
        pltpu.make_async_copy(self.s3, mine, self.d_r).start()
        for p in range(4):

            @pl.when(at.z != p)
            def _(p=p):
                drain(self.s3x.at[p], self.z_s.at[p])

    def end(self):
        drain(self.r4, self.d_r)
        drain(self.r4.at[pl.ds(0, 7)], self.d_s)


def slot_positions(ct):
    me = lax.axis_index("dp")
    table = ct[:, 0, :]
    mine = jnp.where(iota((DP, DP), 1) == me, table, 0).astype(F32)
    counts = jnp.sum(mine, axis=1, keepdims=True)
    source = iota((DP, SLOTS), 0)
    slot_source = iota((DP, SLOTS), 1) // CAP
    start = jnp.sum(jnp.where(source < slot_source, counts, 0.0), axis=0, keepdims=True)
    count = jnp.sum(jnp.where(source == slot_source, counts, 0.0), axis=0, keepdims=True)
    within = lax.rem(iota((1, SLOTS), 1), CAP).astype(F32)
    return jnp.where(within < count, start + within, -1.0)


def compact(pos, rows_ref, out_ref):
    rows = rows_ref[...].reshape(SLOTS, N)
    for chunk in range(2):
        slots = slice(256 * chunk, 256 * chunk + 768)
        index = (iota((256, 768), 0) + 256 * chunk).astype(F32)
        hot = onehot(index == pos[:, slots])
        out_ref[256 * chunk : 256 * chunk + 256] = dot(hot, rows[slots]).astype(BF16)


def centred(values):
    center = values - jnp.mean(values, axis=-1, keepdims=True)
    spread = jnp.mean(center * center, axis=-1, keepdims=True)
    scale = lax.rsqrt(spread + EPSILON)
    return center * scale, scale


def norm_grad(grad, normed, scale):
    lead = jnp.mean(grad, axis=-1, keepdims=True)
    along = jnp.mean(grad * normed, axis=-1, keepdims=True)
    return scale * (grad - lead - normed * along)


def sigmoid(x):
    return 0.5 * jnp.tanh(0.5 * x) + 0.5


def allowed_mask(users, mask):
    row = users[...].astype(F32)
    column = column_of(row, N)
    for b in range(4):
        keys = slice(128 * b, 128 * b + 128)
        same = column == row[:, keys]
        causal = iota((N, 128), 1) + 128 * b <= iota((N, 128), 0)
        mask[:, keys] = onehot(same & causal)


def half_lanes(hh):
    return jnp.where(iota((1, 128), 1) // 64 == hh, 1.0, 0.0)


U, V, Q, K = (slice(128 * i, 128 * i + 128) for i in range(4))


SEEN = ((0, 128), (0, 256), (0, 384), (128, 512))


def clear_unseen(ref):
    zero = jnp.zeros((HEADS, 128, 128), BF16)
    ref[:, 0:128, 128:256] = zero
    ref[:, 256:384, 384:512] = zero
    ref[:, 384:512, 0:128] = zero


def pair_forward(p, xh, wp, mask, act, slope, wt, gs, att):
    for half in range(2):
        cols = slice(256 * half, 256 * half + 256)
        pre = dot(xh[...], wp[p, :, cols])
        sig = sigmoid(pre)
        silu = pre * sig
        act[p, :, cols] = silu.astype(BF16)
        slope[p, :, cols] = (sig + silu * (1.0 - sig)).astype(BF16)
    v, q, k = act[p, :, V], act[p, :, Q], act[p, :, K]
    for t in range(2):
        rows = slice(256 * t, 256 * t + 256)
        nk = 256 * (t + 1)
        total = None
        for hh in range(2):
            lanes = half_lanes(hh)
            qm = q[rows] * lanes.astype(BF16)
            scores = dot_nt(qm, k[:nk])
            for r in range(2):
                first = 256 * t + 128 * r
                part, keys = slice(first, first + 128), slice(*SEEN[2 * t + r])
                half = scores[128 * r : 128 * r + 128, keys] * 0.0625
                th = jnp.tanh(half)
                silu = half + half * th
                sig = 0.5 + 0.5 * th
                grad = (sig + silu * (1.0 - sig)) * 0.125
                ok = mask[part, keys]
                wt[2 * p + hh, part, keys] = silu.astype(BF16) * ok
                gs[2 * p + hh, part, keys] = grad.astype(BF16) * ok
            out = dot(wt[2 * p + hh, rows, :nk], v[:nk]) * lanes
            total = out if total is None else total + out
        att[rows, pl.ds(pl.multiple_of(128 * p, 128), 128)] = total


def pair_backward(p, act, slope, wt, gs, da, dpre):
    v, q, k = act[p, :, V], act[p, :, Q], act[p, :, K]
    d = da[:, pl.ds(pl.multiple_of(128 * p, 128), 128)]
    qt = jnp.transpose(q)
    dt = jnp.transpose(d)
    dvs, dks = [], []
    dq = [None, None]
    for hh in range(2):
        lanes = half_lanes(hh)
        half = slice(64 * hh, 64 * hh + 64)
        dv, dk = [], []
        for t in range(2):
            rows = slice(256 * t, 256 * t + 256)
            nk = 256 * (t + 1)
            dm = d[rows] * lanes.astype(BF16)
            dw = dot_nt(dm, v[:nk])
            ds = (dw * gs[2 * p + hh, rows, :nk].astype(F32)).astype(BF16)
            part = dot(ds, k[:nk]) * lanes
            dq[t] = part if dq[t] is None else dq[t] + part
            dk.append(dot(qt[half, rows], ds))
            dv.append(dot(dt[half, rows], wt[2 * p + hh, rows, :nk]))
        dks.append(jnp.concatenate([dk[0] + dk[1][:, :256], dk[1][:, 256:]], axis=1))
        dvs.append(jnp.concatenate([dv[0] + dv[1][:, :256], dv[1][:, 256:]], axis=1))
    for t in range(2):
        rows = slice(256 * t, 256 * t + 256)
        dpre[p, rows, Q] = dq[t].astype(BF16) * slope[p, rows, Q]
    dk = jnp.transpose(jnp.concatenate(dks, axis=0))
    dv = jnp.transpose(jnp.concatenate(dvs, axis=0))
    dpre[p, :, K] = dk.astype(BF16) * slope[p, :, K]
    dpre[p, :, V] = dv.astype(BF16) * slope[p, :, V]


def gate(att, scale, act, gated):
    for t in range(2):
        rows = slice(256 * t, 256 * t + 256)
        normed, by = centred(att[rows])
        u = jnp.concatenate([act[p, rows, U] for p in range(4)], axis=1).astype(F32)
        gated[rows] = (normed * u).astype(BF16)
        att[rows] = normed
        scale[rows] = jnp.broadcast_to(by, (256, 128))


def gate_grad(att, scale, act, slope, dy, wo, da, dpre):
    for t in range(2):
        rows = slice(256 * t, 256 * t + 256)
        normed = att[rows]
        u = jnp.concatenate([act[p, rows, U] for p in range(4)], axis=1).astype(F32)
        dg = dot_nt(dy[rows], wo[...]).astype(BF16).astype(F32)
        du = (dg * normed).astype(BF16)
        for p in range(4):
            dpre[p, rows, U] = du[:, 128 * p : 128 * p + 128] * slope[p, rows, U]
        da[rows] = norm_grad(dg * u, normed, scale[rows, 0:1]).astype(BF16)


def out_grad(dy, gated, g):
    term = dot(jnp.transpose(dy[...]), gated[...]).astype(BF16)
    for chip in range(CHIPS):
        first = 64 * (chip % 4) + 16 * (chip // 4)
        for c in range(2):
            row = 32 * chip + 16 * c
            for y in range(4):
                g[c, 0, y, first : first + 16, :] = term[row : row + 16, 128 * y : 128 * y + 128]


def pair_in_grad(p, xht, dpre, g):
    for half in range(2):
        term = dot(xht[...], dpre[p, :, 256 * half : 256 * half + 256]).astype(BF16)
        for x in range(2):
            for c in range(2):
                for y in range(4):
                    first = 256 * c + 64 * y
                    row = 64 * (2 * half + x)
                    g[c, 1 + p, y, row : row + 64, :] = term[
                        first : first + 64, 128 * x : 128 * x + 128
                    ]


def row_grad(xn, xscale, dy, dpre, wp, dx):
    for t in range(2):
        rows = slice(256 * t, 256 * t + 256)
        dxh = dot_nt(dpre[0, rows], wp[0])
        for p in range(1, 4):
            dxh = dxh + dot_nt(dpre[p, rows], wp[p])
        dxh = dxh.astype(BF16).astype(F32)
        grad = norm_grad(dxh, xn[rows], xscale[rows, 0:1])
        dx[rows] = (grad + dy[rows].astype(F32)).astype(BF16)


def spread(chunk, column, dx, out):
    part = column[pl.ds(pl.multiple_of(256 * chunk, 256), 256)]
    hot = jnp.concatenate(
        [onehot((iota((256, 128), 1) + 128 * b).astype(F32) == part) for b in range(4)], axis=1
    )
    out[pl.ds(8 * chunk, 8)] = dot(hot, dx[...]).astype(BF16).reshape(8, CAP, N)


def layer_kernel(
    ev_any, go_any, w_any, wo_any, place_any, cnt_any, users_any,
    ret, r4,
    place, cnt, users, ev, go, wp, wo, sx, sy, rx, ry, ct, dxp,
    x, xn, xscale, dy, xh, xht, act, slope, mask, wt, gs, att, scale, da, dpre, gated, dx, column,
    g, r1, s1, r2, s2, r2x, s2x, r2y, s3x, r5, r3z, rwx, s2w, rwy, s3,
    load, xs, xr, ys, yr, cs, cr, bs, br, *sems,
):
    at = Place()
    barrier = pltpu.get_barrier_semaphore()
    small = [
        pltpu.make_async_copy(place_any, place, load.at[0]),
        pltpu.make_async_copy(ev_any, ev, load.at[1]),
        pltpu.make_async_copy(cnt_any, cnt, load.at[2]),
        pltpu.make_async_copy(users_any, users, load.at[3]),
        pltpu.make_async_copy(go_any, go, load.at[4]),
        pltpu.make_async_copy(wo_any, wo, load.at[5]),
    ]
    small[0].start()
    small[1].start()
    for dxo in (2, 1, 3, 0):
        each_peer(at, dxo, lambda peer: signal(barrier, peer, at.rep))
    for i in range(1, REP):
        for c in range(2):
            signal(barrier, at.chip * 2 + c, lax.rem(at.rep + i, REP))
    for copy in small[2:]:
        copy.start()
    for p in range(4):
        for i in range(4):
            pltpu.make_async_copy(
                w_any.at[:, pl.ds(512 * i + 128 * p, 128)],
                wp.at[p, :, pl.ds(128 * i, 128)],
                load.at[6],
            ).start()
    small[0].wait()
    small[1].wait()
    to_x = Exchange(at, sx, rx, xs, xr)
    to_y = Exchange(at, sy, ry, ys, yr)
    counts = Exchange(at, cnt, ct, cs, cr, whole=True)
    back = Exchange(at, dxp, ret, bs, br)
    reduce = Reduce(
        at, (g, r1, s1, r2, s2, r2x, s2x, r2y, s3x, r5, r3z, rwx, s2w, rwy, s3, r4), sems
    )
    columns = (2, 1, 3, 0)
    for dxo in columns:
        pack(lax.rem(at.x + dxo, 4), place, ev, sx)
    small[2].wait()
    pl.semaphore_wait(barrier, DP - 1 + 2 * (REP - 1))
    for dxo in columns:
        counts.start_column(dxo)
    for dxo in columns:
        to_x.start_column(dxo)
    small[4].wait()
    for dxo in columns:
        pack(lax.rem(at.x + dxo, 4), place, go, sy)
    small[3].wait()
    allowed_mask(users, mask)
    clear_unseen(wt)
    clear_unseen(gs)
    counts.wait()
    for dxo in columns:
        to_y.start_column(dxo)
    pos = slot_positions(ct)
    column[...] = column_of(pos, SLOTS)
    small[5].wait()
    drain(wp, load.at[6])
    to_x.wait()
    compact(pos, rx, x)
    normed, by = centred(x[...].astype(F32))
    xn[...] = normed
    xscale[...] = jnp.broadcast_to(by, (N, 128))
    xh[...] = normed.astype(BF16)
    xht[...] = jnp.transpose(xh[...])

    @pl.loop(0, 4)
    def _(p):
        pair_forward(p, xh, wp, mask, act, slope, wt, gs, att)

    gate(att, scale, act, gated)
    to_y.wait()
    compact(pos, ry, dy)
    gate_grad(att, scale, act, slope, dy, wo, da, dpre)
    out_grad(dy, gated, g)
    reduce.pair(0).start()
    for p in range(4):
        pair_backward(p, act, slope, wt, gs, da, dpre)
        pair_in_grad(p, xht, dpre, g)
        reduce.pair(1 + p).start()
        reduce.pair_done(p)
    row_grad(xn, xscale, dy, dpre, wp, dx)
    for dxo in columns:
        spread(lax.rem(at.x + dxo, 4), column, dx, dxp)
        back.start(dxo, (0, 2, 4))
        if dxo == 2:
            reduce.pair_done(4)
    reduce.x_done(0)
    reduce.out_x_start()
    reduce.y_done(2)
    reduce.xy_done(0)
    for dxo in columns:
        back.start(dxo, (6,))
    reduce.x_done(1)
    reduce.out_y_start()
    reduce.y_done(4)
    for dxo in columns:
        back.start(dxo, (1, 5))
    reduce.yx_done(2)
    reduce.xy_done(1)
    for dxo in columns:
        back.start(dxo, (3,))
    reduce.yx_done(4)
    for dxo in columns:
        back.start(dxo, (7,))
    reduce.finish()
    reduce.end()
    back.wait()


def finish_kernel(ret, r4, place, ge_any, gw_any, gout_any, ge, gw, gout, sems):
    core = lax.rem(lax.axis_index("dp"), 2)
    column = column_of(place[...].astype(F32), N)
    stores = []
    for t in range(2):
        rows = slice(256 * t, 256 * t + 256)
        hot = jnp.concatenate(
            [onehot((iota((256, 128), 1) + 128 * b).astype(F32) == column[rows]) for b in range(8)],
            axis=1,
        )
        ge[rows] = dot(hot, ret[...].reshape(SLOTS, N)).astype(BF16)
        part = pl.ds(256 * t, 256)
        stores.append(pltpu.make_async_copy(ge.at[part], ge_any.at[part], sems.at[t]))
        stores[-1].start()
    for c in range(2):
        for half in range(2):
            block = jnp.concatenate([r4[4 * half + c, :64], r4[4 * half + 2 + c, :64]], axis=0)
            block = jnp.transpose(block.astype(F32))
            first = 256 * c + 128 * half
            gw[:, first : first + 128] = jnp.where(core == 1, block[64:], block[:64])
    for y in range(4):
        gout[:, 128 * y : 128 * y + 128] = r4[2 * y + core, 64:80].astype(F32)
    stores.append(pltpu.make_async_copy(gw, gw_any, sems.at[2]))
    stores.append(pltpu.make_async_copy(gout, gout_any, sems.at[3]))
    stores[2].start()
    stores[3].start()
    for copy in stores:
        copy.wait()


DMA = pltpu.SemaphoreType.DMA
BLOCKS = pltpu.VMEM((DP, CAP, N), BF16)
SQUARE = pltpu.VMEM((N, N), BF16)
PAIRS = pltpu.VMEM((4, N, N), BF16)
TERMS = pltpu.VMEM((5, 4, 256, 128), BF16)
COLUMNS = pltpu.VMEM((2, 4, 64, 128), BF16)
SCRATCH = [
    pltpu.VMEM((1, N), I32), pltpu.VMEM((1, DP), I32), pltpu.VMEM((1, N), I32),
    SQUARE, SQUARE, PAIRS, SQUARE,
    BLOCKS, BLOCKS, BLOCKS, BLOCKS, pltpu.VMEM((DP, 1, DP), I32), BLOCKS,
    SQUARE, pltpu.VMEM((N, N), F32), pltpu.VMEM((N, 128), F32),
    SQUARE, SQUARE, SQUARE, PAIRS, PAIRS, SQUARE,
    pltpu.VMEM((HEADS, N, N), BF16), pltpu.VMEM((HEADS, N, N), BF16),
    pltpu.VMEM((N, N), F32), pltpu.VMEM((N, 128), F32),
    SQUARE, PAIRS, SQUARE, SQUARE,
    pltpu.VMEM((SLOTS, 128), F32),
    pltpu.VMEM((2, 5, 4, 256, 128), BF16), TERMS, TERMS, TERMS,
    pltpu.VMEM((5, 256, 128), BF16),
    pltpu.VMEM((3, 4, 4, 64, 128), BF16), pltpu.VMEM((3, 4, 64, 128), BF16), COLUMNS,
    pltpu.VMEM((4, 64, 128), BF16),
    pltpu.VMEM((2, 4, 64, 128), BF16), pltpu.VMEM((4, 64, 128), BF16),
    pltpu.VMEM((4, 4, 16, 128), BF16), pltpu.VMEM((4, 16, 128), BF16),
    pltpu.VMEM((4, 16, 128), BF16), pltpu.VMEM((80, 128), BF16),
    DMA((7,)), DMA, DMA, DMA, DMA, DMA, DMA, DMA, DMA,
    DMA((5,)), DMA((5,)), DMA((5,)), DMA((5,)),
    DMA((3,)), DMA((3,)), DMA((2,)), DMA((2,)), DMA((4,)), DMA,
    DMA((2,)), DMA((2,)), DMA, DMA, DMA, DMA, DMA, DMA,
]
VM = pl.BlockSpec(memory_space=pltpu.VMEM)
ANY = pl.BlockSpec(memory_space=pl.ANY)


def on_device(events, grad_out, w_uvqk, w_out, send_place, send_counts, user_ids):
    ret, r4 = pl.pallas_call(
        layer_kernel,
        name="layer",
        out_shape=(pltpu.VMEM((DP, CAP, N), BF16), pltpu.VMEM((8, 80, 128), BF16)),
        in_specs=[ANY] * 7,
        out_specs=(VM,) * 2,
        scratch_shapes=SCRATCH,
        compiler_params=pltpu.CompilerParams(
            collective_id=0, has_side_effects=True, vmem_limit_bytes=VMEM_LIMIT
        ),
    )(events, grad_out, w_uvqk, w_out, send_place, send_counts, user_ids)
    ge, gw, gout = pl.pallas_call(
        finish_kernel,
        name="finish",
        out_shape=(
            jax.ShapeDtypeStruct((N, N), BF16),
            jax.ShapeDtypeStruct((64, N), F32),
            jax.ShapeDtypeStruct((16, N), F32),
        ),
        in_specs=[VM] * 3,
        out_specs=(ANY,) * 3,
        scratch_shapes=[
            SQUARE, pltpu.VMEM((64, N), F32), pltpu.VMEM((16, N), F32), DMA((4,)),
        ],
        compiler_params=pltpu.CompilerParams(vmem_limit_bytes=16 * 1024 * 1024),
    )(ret, r4, send_place)
    return ge, gw.T, gout.T


def solution(mesh):
    rows = P(("dp", "rep"), None)
    return jax.shard_map(
        on_device,
        mesh=mesh,
        in_specs=(rows, rows, P(), P(), rows, rows, rows),
        out_specs=(rows, P(None, "dp"), P(None, "dp")),
        check_vma=False,
    )
```
